128 devices in a mesh: chan: 16 (over z, y_lo, core), filt: 8 (over x, y_hi).
Axes of the slice: x: 4, y: 4 (y_hi: 2, y_lo: 2; y = y_hi * 2 + y_lo), z: 4, core: 2. Of those that a mesh axis runs over, the one named last changes fastest.
Arguments:
- inputs: bfloat16 [2048, 16, 1024], P('chan', 'filt'), may hold values from -6 to 6
- conv_kernel: bfloat16 [27, 2048, 128], P(None, 'chan'), may hold values from -0.109375 to 0.109375
- proj_weight: bfloat16 [2048, 2048], P('filt', 'chan'), may hold values from -0.1875 to 0.1875
- out_grad: bfloat16 [2048, 16, 1024], P('chan', 'filt'), may hold values from -6 to 6
Outputs:
- projected: bfloat16 [2048, 16, 1024], P('chan', 'filt')
- input_grad: bfloat16 [2048, 16, 1024], P('chan', 'filt')
- kernel_grad: float32 [27, 2048, 128], P(None, 'chan')
- weight_grad: float32 [2048, 2048], P('filt', 'chan')
The draws below stay inside these ranges and needn't reach their ends.
All inputs are finite; a program needn't handle non-finite values.
Results may differ from the reference program's by a relative error of at most 0.018.
Values may be sent and summed in bfloat16 or wider, within the bound.
A program may use at most 128 MiB of HBM per device.

```python
import jax
import jax.numpy as jnp
from jax import lax

G = 128
NY = 32
NZ = 32
C = 2048
F = 2048
NX = 16
YZ = 1024


def spiked(entries, rng, source, target, blocks, factor):
    def block_of(axis_at):
        return (jnp.arange(entries.shape[axis_at]) // (entries.shape[axis_at] // blocks)).reshape((-1,) + (1,) * (entries.ndim - 1 - axis_at))

    first = jax.random.permutation(rng, blocks)[block_of(target)]
    far = (block_of(target) + blocks // 2) % blocks
    return jnp.where((block_of(source) == first) | (block_of(source) == far), factor * entries, entries)


def level_of(rng, shape, cuts, smallest, high):
    gain = 1.0
    for axis_at, shards_of in cuts:
        draws = jax.random.uniform(jax.random.fold_in(jax.random.fold_in(rng, 6), axis_at), (shards_of,), jnp.float32, smallest / len(cuts), high / len(cuts))
        gain = gain * jnp.repeat(jnp.exp(draws), shape[axis_at] // shards_of).reshape((-1,) + (1,) * (len(shape) - 1 - axis_at))
    return gain


def gaussian(rng, dims, scale, most, pieces=(), held_as=jnp.bfloat16):
    loudness = level_of(rng, dims, pieces, -0.22, 0.18) if pieces else 1.0
    values = jax.random.normal(rng, dims, jnp.float32) * scale * loudness
    return jnp.minimum(jnp.maximum(values, -most), most).astype(held_as)


def gaussian_with(own_key, dims, deviation, reach, cuts, heavy, dtype=jnp.bfloat16):
    drawn = deviation * jax.random.normal(own_key, dims, jnp.float32)
    if cuts:
        drawn = drawn * level_of(own_key, dims, cuts, -0.22, 0.18)
    return jnp.clip(spiked(drawn, jax.random.fold_in(own_key, 3), *heavy), -reach, reach).astype(dtype)


def setup_inputs(seed: int = 0) -> dict:
    keys = jax.random.split(jax.random.key(seed), 5)
    inputs = gaussian(keys[0], (C, NX, YZ), 1.0, 6.0, ((0, 16), (1, 8)))
    conv_kernel = gaussian(keys[1], (27, C, G), (27 * G) ** -0.5, 0.109375, ((1, 16),))
    proj_weight = gaussian_with(keys[2], (F, C), C ** -0.5, 0.1875, ((0, 8), (1, 16)), (1, 0, 16, 2.0))
    out_grad = gaussian(keys[3], (F, NX, YZ), 1.0, 6.0, ((0, 16), (1, 8)))
    return {"inputs": inputs, "conv_kernel": conv_kernel, "proj_weight": proj_weight, "out_grad": out_grad}


def activation(values):
    return jax.nn.gelu(values, approximate=True)


def tap_list():
    result = []
    for shift_a in (-1, 0, 1):
        for shift_b in (-1, 0, 1):
            for shift_c in (-1, 0, 1):
                result.append((shift_a, shift_b, shift_c))
    return result


def reference(inputs, conv_kernel, proj_weight, out_grad):
    groups = C // G
    volume = inputs.astype(jnp.float32).reshape(C, NX, NY, NZ)
    padded = jnp.pad(volume, ((0, 0), (1, 1), (1, 1), (1, 1)))
    pre = jnp.zeros((groups, G, NX * NY * NZ), jnp.float32)
    for tap, (shift_a, shift_b, shift_c) in enumerate(tap_list()):
        window = padded[:, 1 + shift_a:1 + shift_a + NX, 1 + shift_b:1 + shift_b + NY, 1 + shift_c:1 + shift_c + NZ].reshape(groups, G, -1)
        kernel_tap = conv_kernel[tap].astype(jnp.float32).reshape(groups, G, G)
        pre = pre + jnp.einsum('gok,gkn->gon', kernel_tap, window)
    pre = pre.reshape(C, -1)
    hidden = activation(pre).astype(jnp.bfloat16)
    projected = jnp.zeros((F, NX * NY * NZ), jnp.float32)
    for group in range(groups):
        term = jnp.dot(proj_weight[:, group * G:(group + 1) * G], hidden[group * G:(group + 1) * G], preferred_element_type=jnp.float32)
        rounded = lax.optimization_barrier(term.astype(jnp.bfloat16))
        projected = projected + rounded.astype(jnp.float32)
    projected = projected.astype(jnp.bfloat16)
    grad_flat = out_grad.reshape(F, -1)
    hidden_grad = jnp.dot(proj_weight.T, grad_flat, preferred_element_type=jnp.float32)
    weight_grad = jnp.dot(grad_flat, hidden.T, preferred_element_type=jnp.float32)
    derivative = jax.jvp(activation, (pre,), (jnp.ones_like(pre),))[1]
    conv_grad = (hidden_grad * derivative).astype(jnp.bfloat16)
    grad_float = conv_grad.astype(jnp.float32)
    grad_pad = jnp.pad(grad_float.reshape(C, NX, NY, NZ), ((0, 0), (1, 1), (1, 1), (1, 1)))
    grad_groups = grad_float.reshape(groups, G, -1)
    input_grad = jnp.zeros((groups, G, NX * NY * NZ), jnp.float32)
    kernel_parts = []
    for tap, (shift_a, shift_b, shift_c) in enumerate(tap_list()):
        kernel_tap = conv_kernel[tap].astype(jnp.float32).reshape(groups, G, G)
        moved = grad_pad[:, 1 - shift_a:1 - shift_a + NX, 1 - shift_b:1 - shift_b + NY, 1 - shift_c:1 - shift_c + NZ].reshape(groups, G, -1)
        input_grad = input_grad + jnp.einsum('gok,gon->gkn', kernel_tap, moved)
        window = padded[:, 1 + shift_a:1 + shift_a + NX, 1 + shift_b:1 + shift_b + NY, 1 + shift_c:1 + shift_c + NZ].reshape(groups, G, -1)
        kernel_parts.append(jnp.einsum('gon,gkn->gok', grad_groups, window).reshape(C, G))
    kernel_grad = jnp.stack(kernel_parts, axis=0)
    input_grad = input_grad.reshape(C, NX, NY * NZ).astype(jnp.bfloat16)
    return projected.reshape(F, NX, NY * NZ), input_grad, kernel_grad, weight_grad
```

```python
import jax
import jax.numpy as jnp
from jax import lax
from jax.experimental import pallas as pl
from jax.experimental.pallas import tpu as pltpu
from jax.sharding import PartitionSpec as P

MESH = pl.DeviceIdType.MESH
F32 = jnp.float32
BF16 = jnp.bfloat16
NN = (((1,), (0,)), ((), ()))
NT = (((1,), (1,)), ((), ()))
N_SEMS = 128


def dot(a, b, dims):
    return lax.dot_general(a, b, dims, preferred_element_type=F32)


def kernel(
    x_ref, k_ref, w_ref, o_ref,
    p_out, ig_out, kg_out, wg_out,
    obuf, xhalo, x3t, k3, wbuf, wt, hown, hbuf, der,
    pbuf, r1, r2, r3, p4, r4,
    ghb, ghs, ghr, cg, cgt, chalo, c3t,
    wgf, wgs, wgr, wgp, wgq,
    kgb, kgr, kgs, kgall,
    ssem, rsem,
):
    ch = lax.axis_index("chan")
    fi = lax.axis_index("filt")
    co = ch % 2
    q = ch // 2
    yl = q % 2
    z = q // 2
    sib = ch + 1 - 2 * co
    zp = (ch + 4) % 16
    zm = (ch + 12) % 16
    yn = ch + 2 - 4 * yl
    own, oth = co, 1 - co
    flip = 1 - 2 * yl
    q_zp = ((z + 1) % 4) * 2 + yl
    q_zm = ((z + 3) % 4) * 2 + yl
    q_z2 = ((z + 2) % 4) * 2 + yl
    others = [(fi + d) % 8 for d in range(1, 8)]
    sent = []

    def send(src, dst, chan_id, filt_id=None):
        i = len(sent)
        copy = pltpu.make_async_remote_copy(
            src_ref=src, dst_ref=dst, send_sem=ssem.at[i], recv_sem=rsem.at[i],
            device_id=(chan_id, fi if filt_id is None else filt_id), device_id_type=MESH,
        )
        copy.start()
        sent.append(copy)
        return copy

    barrier = pltpu.get_barrier_semaphore()
    for c in (sib, zp, zm, yn):
        pl.semaphore_signal(barrier, inc=1, device_id=(c, fi), device_id_type=MESH)
    for f in others:
        pl.semaphore_signal(barrier, inc=1, device_id=(ch, f), device_id_type=MESH)
    pl.semaphore_wait(barrier, 11)

    c1 = send(o_ref.at[oth], obuf.at[q, own], sib)
    a_p = send(o_ref.at[own], obuf.at[q, own], zp)
    a_m = send(o_ref.at[own], obuf.at[q, own], zm)
    a_y = send(o_ref.at[own], obuf.at[q, own], yn)
    x_up = send(x_ref.at[1], xhalo.at[0], ch, (fi + 1) % 8)
    x_dn = send(x_ref.at[0], xhalo.at[1], ch, (fi + 7) % 8)
    w_own = pl.ds(pl.multiple_of(fi * 256, 256), 256)
    w_out = [send(w_ref, wbuf.at[own, w_own], ch, f) for f in others]
    w_sib = [send(w_ref, wbuf.at[own, w_own], sib)]

    wbuf[own, w_own] = w_ref[...]
    obuf[q, own] = o_ref[own]
    for t in range(27):
        k3[:, t * 128 : (t + 1) * 128] = k_ref[t]

    def spread(dst, at, src, low, keep):
        edge = jnp.zeros((32, 384), BF16)
        dst[at, 0:32] = edge
        dst[at, 1056:1088] = edge

        @pl.loop(0, 4)
        def _(i):
            rows = pl.ds(pl.multiple_of(i * 256, 256), 256)
            v = src[rows].astype(F32) * keep
            r = lax.broadcasted_iota(jnp.int32, (256, 128), 0) % 32
            prev = jnp.where(r == 0, 0.0, pltpu.roll(v, 1, 0))
            after = jnp.where(r == 31, 0.0, pltpu.roll(v, 255, 0))
            left, right = (prev, after) if low else (after, prev)
            to = pl.ds(pl.multiple_of(i * 256 + 32, 32), 256)
            dst[at, to, 0:128] = left.astype(BF16)
            dst[at, to, 128:256] = v.astype(BF16)
            dst[at, to, 256:384] = right.astype(BF16)

    one = jnp.float32(1.0)
    first = jnp.where(fi == 0, 0.0, 1.0).astype(F32)
    last = jnp.where(fi == 7, 0.0, 1.0).astype(F32)
    spread(x3t, 1, x_ref.at[0], True, one)
    spread(x3t, 2, x_ref.at[1], True, one)

    c1.wait_recv()
    b_y = send(obuf.at[q, oth], obuf.at[q, oth], yn)
    b_p = send(obuf.at[q, oth], obuf.at[q, oth], zp)
    b_m = send(obuf.at[q, oth], obuf.at[q, oth], zm)

    for d, c in enumerate(w_out):
        c.wait_recv()
        src = (fi + 7 - d) % 8
        rows = pl.ds(pl.multiple_of(src * 256, 256), 256)
        w_sib.append(send(wbuf.at[own, rows], wbuf.at[own, rows], sib))

    x_up.wait_recv()
    x_dn.wait_recv()
    spread(x3t, 0, xhalo.at[0], True, first)
    spread(x3t, 3, xhalo.at[1], True, last)

    lower, upper = pl.ds(0, 64), pl.ds(64, 64)
    a_p.wait_recv()
    af_p = send(obuf.at[q_zm, own, lower], obuf.at[q_zm, own, lower], zp)
    ay_m = send(obuf.at[q_zm, own], obuf.at[q_zm, own], yn)
    a_m.wait_recv()
    af_m = send(obuf.at[q_zp, own, upper], obuf.at[q_zp, own, upper], zm)
    ay_p = send(obuf.at[q_zp, own], obuf.at[q_zp, own], yn)

    def convolve(plane, count, start):
        @pl.loop(start, start + count)
        def _(i):
            cols = pl.ds(pl.multiple_of(i * 256, 256), 256)
            wins = [
                x3t[plane + a, pl.ds(pl.multiple_of(i * 256 + 32 * b, 32), 256)]
                for a in range(3) for b in range(3)
            ]
            v = dot(k3[...], jnp.concatenate(wins, axis=1), NT)
            s = 0.7978845608028654
            sq = v * v
            t = jnp.tanh(s * (v + 0.044715 * sq * v))
            hown[plane, :, cols] = (0.5 * v * (1.0 + t)).astype(BF16)
            der[plane, :, cols] = 0.5 * (1.0 + t) + 0.5 * v * (1.0 - t * t) * (
                s * (1.0 + 3 * 0.044715 * sq)
            )

    convolve(oth, 2, 0)
    b_y.wait_recv()
    b2_p = send(obuf.at[q + flip, oth], obuf.at[q + flip, oth], zp)
    b2_m = send(obuf.at[q + flip, oth], obuf.at[q + flip, oth], zm)
    convolve(oth, 2, 2)
    h_x = send(hown.at[oth], hbuf.at[own], sib)
    b_p.wait_recv()
    bf_p = send(obuf.at[q_zm, oth, lower], obuf.at[q_zm, oth, lower], zp)
    b_m.wait_recv()
    bf_m = send(obuf.at[q_zp, oth, upper], obuf.at[q_zp, oth, upper], zm)
    convolve(own, 2, 0)
    af_p.wait_recv()
    af_m.wait_recv()
    ay_2 = send(obuf.at[q_z2, own], obuf.at[q_z2, own], yn)
    convolve(own, 2, 2)
    hbuf[own] = hown[own]
    b2_p.wait_recv()
    b2f_p = send(obuf.at[q_zm + flip, oth, lower], obuf.at[q_zm + flip, oth, lower], zp)
    b2_m.wait_recv()
    b2f_m = send(obuf.at[q_zp + flip, oth, upper], obuf.at[q_zp + flip, oth, upper], zm)

    for c in w_sib:
        c.wait_recv()

    @pl.loop(0, 8)
    def _(j):
        rows = pl.ds(pl.multiple_of(j * 256, 256), 256)
        for half in range(2):
            block = wbuf[half, rows].astype(F32)
            wt[half * 128 : (half + 1) * 128, rows] = block.T.astype(BF16)

    h_x.wait_recv()

    def project(at):
        rows = pl.ds(pl.multiple_of(at * 256, 256), 256)
        w = jnp.concatenate([wbuf[0, rows], wbuf[1, rows]], axis=1)

        @pl.loop(0, 4)
        def _(i):
            cols = pl.ds(pl.multiple_of(i * 256, 256), 256)
            h = jnp.concatenate([hbuf[0, :, cols], hbuf[1, :, cols]], axis=0)
            v = dot(w, h, NN).astype(BF16)
            pbuf[at, 0, :, cols] = v[:128]
            pbuf[at, 1, :, cols] = v[128:]

    far = (q_z2, q_z2 + flip)
    up = (q_zp, q_zp + flip)
    down = (q_zm, q_zm + flip)
    here = (q, q + flip)
    for at in far:
        project(at)
    s1 = []
    for i in range(2):
        s1.append((
            send(pbuf.at[far[i], 0], r1.at[0, i], zp),
            send(pbuf.at[far[i], 1], r1.at[1, i], zm),
        ))
    for at in up + down + here:
        project(at)

    for c in (a_y, ay_m, ay_p, ay_2, bf_p, bf_m, b2f_p, b2f_m):
        c.wait_recv()

    @pl.loop(0, 4)
    def _(i):
        cols = pl.ds(pl.multiple_of(i * 256, 256), 256)
        o = obuf[:, :, :, cols].reshape(2048, 256)
        v = dot(wt[...], o, NN)
        ghb[0, :, cols] = v[:128]
        ghb[1, :, cols] = v[128:]

    ghs[...] = ghb[oth].astype(BF16)
    g_x = send(ghs, ghr, sib)

    s2 = []
    for i in range(2):
        for side, blocks in ((0, up), (1, down)):
            s1[i][side].wait_recv()

            pbuf[blocks[i], side] = (
                pbuf[blocks[i], side].astype(F32) + r1[side, i].astype(F32)
            ).astype(BF16)
        s2.append((
            send(pbuf.at[up[i]], r2.at[0, i], zp),
            send(pbuf.at[down[i]], r2.at[1, i], zm),
        ))

    cg[own] = (ghb[own] * der[own]).astype(BF16)
    g_x.wait_recv()
    cg[oth] = (ghr[...].astype(F32) * der[oth]).astype(BF16)

    for plane in range(2):
        @pl.loop(0, 4)
        def _(i):
            cols = pl.ds(pl.multiple_of(i * 256, 256), 256)
            cgt[plane, cols] = cg[plane, :, cols].astype(F32).T.astype(BF16)

    g_up = send(cgt.at[1], chalo.at[0], ch, (fi + 1) % 8)
    g_dn = send(cgt.at[0], chalo.at[1], ch, (fi + 7) % 8)

    ks = []
    for a in range(3):
        @pl.loop(0, 3)
        def _(b):
            rows = pl.ds(pl.multiple_of(32 * b, 32), 1024)
            v = dot(cg[0], x3t[a, rows], NN) + dot(cg[1], x3t[a + 1, rows], NN)
            for c in range(3):
                to = pl.ds(pl.multiple_of((3 * b + c) * 128, 128), 128)
                kgb[a, to] = v[:, c * 128 : (c + 1) * 128].astype(BF16)

        ks.append([
            send(kgb.at[a, pl.ds(pl.multiple_of(f * 144, 16), 144)], kgr.at[a, fi], ch, f)
            for f in others
        ])

    @pl.loop(0, 8)
    def _(j):
        h = jnp.concatenate([hbuf[0], hbuf[1]], axis=0)
        v = dot(obuf[j].reshape(256, 1024), h, NT)
        lo, hi = v[:, :128], v[:, 128:]
        wgf[j] = jnp.where(co == 0, lo, hi)
        wgs[j] = jnp.where(co == 0, hi, lo).astype(BF16)

    wg_x = send(wgs, wgr, sib)

    spread(c3t, 1, cgt.at[0], False, one)
    spread(c3t, 2, cgt.at[1], False, one)

    for i in range(2):
        s2[i][0].wait_recv()
        s2[i][1].wait_recv()
    pbuf[here[1]] = (
        pbuf[here[1]].astype(F32) + r2[0, 1].astype(F32) + r2[1, 1].astype(F32)
    ).astype(BF16)
    s3 = send(pbuf.at[here[1]], r3, yn)

    wg_x.wait_recv()
    wgf[...] = wgf[...] + wgr[...].astype(F32)
    wgp[...] = wgf[...].astype(BF16)
    wq = [send(wgp.at[f], wgq.at[fi], ch, f) for f in others]

    g_up.wait_recv()
    g_dn.wait_recv()
    spread(c3t, 0, chalo.at[0], False, first)
    spread(c3t, 3, chalo.at[1], False, last)

    def back(plane):
        @pl.loop(0, 4)
        def _(i):
            wins = [
                c3t[plane + 2 - a, pl.ds(pl.multiple_of(i * 256 + 32 * (2 - b), 32), 256)]
                for a in range(3) for b in range(3)
            ]
            v = dot(jnp.concatenate(wins, axis=1), k_ref[...].reshape(3456, 128), NN)
            rows = pl.ds(pl.multiple_of(i * 256, 256), 256)
            ig_out[plane, rows] = v.astype(BF16)

    own_rows = pl.ds(pl.multiple_of(fi * 144, 16), 144)

    def reduce_kernel(a):
        total = kgb[a, own_rows].astype(F32)
        for c in ks[a]:
            c.wait_recv()
        for d in range(1, 8):
            total = total + kgr[a, (fi + d) % 8].astype(F32)
        kgs[a] = total.astype(BF16)
        kgall[a, own_rows] = kgs[a]
        return [send(kgs.at[a], kgall.at[a, own_rows], ch, f) for f in others]

    kq = [reduce_kernel(0)]
    back(0)
    kq.append(reduce_kernel(1))
    kq.append(reduce_kernel(2))

    s3.wait_recv()
    for half in range(2):
        p4[half] = (
            pbuf[here[0], half].astype(F32) + r2[0, 0, half].astype(F32)
            + r2[1, 0, half].astype(F32) + r3[half].astype(F32)
        ).astype(BF16)
    s4 = send(p4.at[oth], r4, sib)
    back(1)
    p_out[own] = p4[own]

    total = wgf[fi]
    for c in wq:
        c.wait_recv()
    for d in range(1, 8):
        total = total + wgq[(fi + d) % 8].astype(F32)
    wg_out[...] = total
    s4.wait_recv()
    p_out[oth] = r4[...]

    for a in range(3):
        for c in kq[a]:
            c.wait_recv()
        kg_out[9 * a : 9 * a + 9] = kgall[a].astype(F32).reshape(9, 128, 128)
    for c in sent:
        c.wait_send()


def body(inputs, conv_kernel, proj_weight, out_grad):
    x = inputs.transpose(1, 2, 0)
    o = out_grad.transpose(1, 0, 2)
    vmem = pl.BlockSpec(memory_space=pltpu.VMEM)
    shapes = [
        ((8, 2, 128, 1024), BF16),
        ((2, 1024, 128), BF16),
        ((4, 1088, 384), BF16),
        ((128, 3456), BF16),
        ((2, 2048, 128), BF16),
        ((256, 2048), BF16),
        ((2, 128, 1024), BF16),
        ((2, 128, 1024), BF16),
        ((2, 128, 1024), F32),
        ((8, 2, 128, 1024), BF16),
        ((2, 2, 128, 1024), BF16),
        ((2, 2, 2, 128, 1024), BF16),
        ((2, 128, 1024), BF16),
        ((2, 128, 1024), BF16),
        ((128, 1024), BF16),
        ((2, 128, 1024), F32),
        ((128, 1024), BF16),
        ((128, 1024), BF16),
        ((2, 128, 1024), BF16),
        ((2, 1024, 128), BF16),
        ((2, 1024, 128), BF16),
        ((4, 1088, 384), BF16),
        ((8, 256, 128), F32),
        ((8, 256, 128), BF16),
        ((8, 256, 128), BF16),
        ((8, 256, 128), BF16),
        ((8, 256, 128), BF16),
        ((3, 1152, 128), BF16),
        ((3, 8, 144, 128), BF16),
        ((3, 144, 128), BF16),
        ((3, 1152, 128), BF16),
    ]
    projected, input_grad, kernel_grad, weight_grad = pl.pallas_call(
        kernel,
        out_shape=(
            jax.ShapeDtypeStruct((2, 128, 1024), BF16),
            jax.ShapeDtypeStruct((2, 1024, 128), BF16),
            jax.ShapeDtypeStruct((27, 128, 128), F32),
            jax.ShapeDtypeStruct((256, 128), F32),
        ),
        in_specs=[vmem] * 4,
        out_specs=(vmem,) * 4,
        scratch_shapes=[pltpu.VMEM(s, d) for s, d in shapes]
        + [pltpu.SemaphoreType.DMA((N_SEMS,)), pltpu.SemaphoreType.DMA((N_SEMS,))],
        compiler_params=pltpu.CompilerParams(
            collective_id=0, has_side_effects=True, vmem_limit_bytes=56 * 1024 * 1024
        ),
    )(x, conv_kernel, proj_weight, o)
    return (
        projected.transpose(1, 0, 2), input_grad.transpose(2, 0, 1), kernel_grad, weight_grad
    )


def solution(mesh):
    in_specs = (
        P("chan", "filt", None),
        P(None, "chan", None),
        P("filt", "chan"),
        P("chan", "filt", None),
    )
    out_specs = (
        P("chan", "filt", None),
        P("chan", "filt", None),
        P(None, "chan", None),
        P("filt", "chan"),
    )
    return jax.shard_map(body, mesh=mesh, in_specs=in_specs, out_specs=out_specs, check_vma=False)
```

```python
import jax
import jax.numpy as jnp
from jax import lax
from jax.experimental import pallas as pl
from jax.experimental.pallas import tpu as pltpu
from jax.sharding import PartitionSpec as P

MESH = pl.DeviceIdType.MESH
F32 = jnp.float32
BF16 = jnp.bfloat16
NN = (((1,), (0,)), ((), ()))
NT = (((1,), (1,)), ((), ()))
N_SEMS = 128


def dot(a, b, dims):
    return lax.dot_general(a, b, dims, preferred_element_type=F32)


def kernel(
    x_ref, k_ref, w_ref, o_ref,
    p_out, ig_out, kg_out, wg_out,
    obuf, xhalo, x3t, k3, wbuf, wt, hown, hbuf, der,
    pbuf, r1, r2, r3, p4, r4,
    ghb, ghs, ghr, cg, cgt, chalo, c3t, kback,
    wgf, wgs, wgr, wgp, wgq, wgy, wgz,
    kgf, kgb, kgr, kgs, kgy, kgall,
    ssem, rsem,
):
    ch = lax.axis_index("chan")
    fi = lax.axis_index("filt")
    co = ch % 2
    q = ch // 2
    yl = q % 2
    z = q // 2
    sib = ch + 1 - 2 * co
    zp = (ch + 4) % 16
    zm = (ch + 12) % 16
    yn = ch + 2 - 4 * yl
    own, oth = co, 1 - co
    flip = 1 - 2 * yl
    q_zp = ((z + 1) % 4) * 2 + yl
    q_zm = ((z + 3) % 4) * 2 + yl
    q_z2 = ((z + 2) % 4) * 2 + yl
    fx = fi // 2
    fy = fi + 1 - 2 * (fi % 2)
    f_up, f_dn = (fi + 1) % 8, (fi + 7) % 8
    fxs = [(fi + 2 * d) % 8 for d in range(1, 4)]
    sent = []

    def send(src, dst, chan_id, filt_id=None):
        i = len(sent)
        copy = pltpu.make_async_remote_copy(
            src_ref=src, dst_ref=dst, send_sem=ssem.at[i], recv_sem=rsem.at[i],
            device_id=(chan_id, fi if filt_id is None else filt_id), device_id_type=MESH,
        )
        copy.start()
        sent.append(copy)
        return copy

    def pass_on(ref, chan_id):
        return send(ref, ref, chan_id)

    barrier = pltpu.get_barrier_semaphore()
    for c in (sib, zp, zm, yn):
        pl.semaphore_signal(barrier, inc=1, device_id=(c, fi), device_id_type=MESH)
    for f in [f_up, f_dn] + fxs:
        pl.semaphore_signal(barrier, inc=1, device_id=(ch, f), device_id_type=MESH)
    pl.semaphore_wait(barrier, 9)

    c1 = send(o_ref.at[oth], obuf.at[q, own], sib)
    a_p = send(o_ref.at[own], obuf.at[q, own], zp)
    a_m = send(o_ref.at[own], obuf.at[q, own], zm)
    a_y = send(o_ref.at[own], obuf.at[q, own], yn)

    def block_of(f):
        return pl.ds(pl.multiple_of(f * 256, 256), 256)

    w_y = send(w_ref, wbuf.at[own, block_of(fi)], ch, fy)
    w_in = [send(w_ref, wbuf.at[own, block_of(fi)], ch, f) for f in fxs]

    wbuf[own, block_of(fi)] = w_ref[...]
    obuf[q, own] = o_ref[own]
    for t in range(27):
        a, lane = t // 9, (t % 9) * 128
        tap = k_ref[t]
        if a > 0:
            k3[0:128, (a - 1) * 1152 + lane : (a - 1) * 1152 + lane + 128] = tap
        if a < 2:
            k3[128:256, a * 1152 + lane : a * 1152 + lane + 128] = tap
        if a == 0:
            k3[0:128, 2304 + lane : 2304 + lane + 128] = tap
        if a == 2:
            k3[128:256, 2304 + lane : 2304 + lane + 128] = tap

    c1.wait_recv()
    b_y = pass_on(obuf.at[q, oth], yn)
    b_p = pass_on(obuf.at[q, oth], zp)
    b_m = pass_on(obuf.at[q, oth], zm)

    def spread(dst, at, src, low, keep):
        edge = jnp.zeros((32, 384), BF16)
        dst[at, 0:32] = edge
        dst[at, 1056:1088] = edge

        @pl.loop(0, 4)
        def _(i):
            rows = pl.ds(pl.multiple_of(i * 256, 256), 256)
            v = src[rows].astype(F32) * keep
            r = lax.broadcasted_iota(jnp.int32, (256, 128), 0) % 32
            prev = jnp.where(r == 0, 0.0, pltpu.roll(v, 1, 0))
            after = jnp.where(r == 31, 0.0, pltpu.roll(v, 255, 0))
            left, right = (prev, after) if low else (after, prev)
            to = pl.ds(pl.multiple_of(i * 256 + 32, 32), 256)
            dst[at, to, 0:128] = left.astype(BF16)
            dst[at, to, 128:256] = v.astype(BF16)
            dst[at, to, 256:384] = right.astype(BF16)

    one = jnp.float32(1.0)
    first = jnp.where(fi == 0, 0.0, 1.0).astype(F32)
    last = jnp.where(fi == 7, 0.0, 1.0).astype(F32)
    spread(x3t, 1, x_ref.at[0], True, one)
    spread(x3t, 2, x_ref.at[1], True, one)

    lower, upper = pl.ds(0, 64), pl.ds(64, 64)
    a_y.wait_recv()
    ya_p = pass_on(obuf.at[q + flip, own], zp)
    ya_m = pass_on(obuf.at[q + flip, own], zm)
    x_up = send(x_ref.at[1], xhalo.at[0], ch, f_up)
    x_dn = send(x_ref.at[0], xhalo.at[1], ch, f_dn)
    w_y.wait_recv()
    w_in += [
        send(wbuf.at[own, block_of(fy)], wbuf.at[own, block_of(fy)], ch, f) for f in fxs
    ]
    a_p.wait_recv()
    forwards = [pass_on(obuf.at[q_zm, own, lower], zp)]
    a_m.wait_recv()
    forwards.append(pass_on(obuf.at[q_zp, own, upper], zm))

    def windows(src, plane, i, order):
        return [
            src[plane, pl.ds(pl.multiple_of(i * 256 + 32 * b, 32), 256)] for b in order
        ]

    def convolve(start, stop):
        @pl.loop(start, stop)
        def _(i):
            cols = pl.ds(pl.multiple_of(i * 256, 256), 256)
            wins = windows(x3t, 1, i, range(3)) + windows(x3t, 2, i, range(3))
            v = dot(k3[:, 0:2304], jnp.concatenate(wins, axis=1), NT)
            der[0, :, cols] = v[:128]
            der[1, :, cols] = v[128:]

    def activate(plane):
        @pl.loop(0, 4)
        def _(i):
            cols = pl.ds(pl.multiple_of(i * 256, 256), 256)
            wins = windows(x3t, 3 * plane, i, range(3))
            taps = k3[pl.ds(pl.multiple_of(plane * 128, 128), 128), 2304:3456]
            v = der[plane, :, cols] + dot(taps, jnp.concatenate(wins, axis=1), NT)
            s = 0.7978845608028654
            sq = v * v
            t = jnp.tanh(s * (v + 0.044715 * sq * v))
            hown[plane, :, cols] = (0.5 * v * (1.0 + t)).astype(BF16)
            der[plane, :, cols] = 0.5 * (1.0 + t) + 0.5 * v * (1.0 - t * t) * (
                s * (1.0 + 3 * 0.044715 * sq)
            )

    convolve(0, 2)
    b_y.wait_recv()
    yb_p = pass_on(obuf.at[q + flip, oth], zp)
    yb_m = pass_on(obuf.at[q + flip, oth], zm)
    b_p.wait_recv()
    forwards.append(pass_on(obuf.at[q_zm, oth, lower], zp))
    b_m.wait_recv()
    forwards.append(pass_on(obuf.at[q_zp, oth, upper], zm))
    convolve(2, 4)
    for c in w_in:
        c.wait_recv()
    w_sib = send(wbuf.at[own], wbuf.at[own], sib)

    x_up.wait_recv()
    x_dn.wait_recv()
    spread(x3t, 0, xhalo.at[0], True, first)
    spread(x3t, 3, xhalo.at[1], True, last)
    activate(oth)
    h_x = send(hown.at[oth], hbuf.at[own], sib)
    ya_p.wait_recv()
    forwards.append(pass_on(obuf.at[q_zm + flip, own, lower], zp))
    ya_m.wait_recv()
    forwards.append(pass_on(obuf.at[q_zp + flip, own, upper], zm))
    activate(own)
    hbuf[own] = hown[own]

    w_sib.wait_recv()

    @pl.loop(0, 8)
    def _(j):
        rows = block_of(j)
        for half in range(2):
            block = wbuf[half, rows].astype(F32)
            wt[half * 128 : (half + 1) * 128, rows] = block.T.astype(BF16)

    yb_p.wait_recv()
    forwards.append(pass_on(obuf.at[q_zm + flip, oth, lower], zp))
    yb_m.wait_recv()
    forwards.append(pass_on(obuf.at[q_zp + flip, oth, upper], zm))
    h_x.wait_recv()

    def project(at):
        rows = block_of(at)
        w = jnp.concatenate([wbuf[0, rows], wbuf[1, rows]], axis=1)

        @pl.loop(0, 4)
        def _(i):
            cols = pl.ds(pl.multiple_of(i * 256, 256), 256)
            h = jnp.concatenate([hbuf[0, :, cols], hbuf[1, :, cols]], axis=0)
            v = dot(w, h, NN).astype(BF16)
            pbuf[at, 0, :, cols] = v[:128]
            pbuf[at, 1, :, cols] = v[128:]

    far = (q_z2 + flip, q_z2)
    up = (q_zp + flip, q_zp)
    down = (q_zm + flip, q_zm)
    here = (q + flip, q)
    for at in far + up + down + here:
        project(at)

    for c in forwards:
        c.wait_recv()
    s1 = [
        (send(pbuf.at[far[i], 0], r1.at[0, i], zp), send(pbuf.at[far[i], 1], r1.at[1, i], zm))
        for i in range(2)
    ]

    @pl.loop(0, 4)
    def _(i):
        cols = pl.ds(pl.multiple_of(i * 256, 256), 256)
        o = obuf[:, :, :, cols].reshape(2048, 256)
        v = dot(wt[...], o, NN)
        ghb[0, :, cols] = v[:128]
        ghb[1, :, cols] = v[128:]

    ghs[...] = ghb[oth].astype(BF16)
    g_x = send(ghs, ghr, sib)

    def to_grad(plane, source):
        @pl.loop(0, 4)
        def _(i):
            cols = pl.ds(pl.multiple_of(i * 256, 256), 256)
            v = (source[:, cols].astype(F32) * der[plane, :, cols]).astype(BF16)
            cg[plane, :, cols] = v
            cgt[plane, cols] = v.astype(F32).T.astype(BF16)

    to_grad(own, ghb.at[own])
    g_x.wait_recv()
    to_grad(oth, ghr)
    g_up = send(cgt.at[1], chalo.at[0], ch, f_up)
    g_dn = send(cgt.at[0], chalo.at[1], ch, f_dn)

    def second(i):
        for side, block in ((0, up[i]), (1, down[i])):
            s1[i][side].wait_recv()
            pbuf[block, side] = (
                pbuf[block, side].astype(F32) + r1[side, i].astype(F32)
            ).astype(BF16)
        return (
            send(pbuf.at[up[i]], r2.at[0, i], zp), send(pbuf.at[down[i]], r2.at[1, i], zm)
        )

    s2 = [second(0)]

    def window_row(plane):
        return jnp.concatenate([x3t[plane, 32 * b : 32 * b + 1024] for b in range(3)], axis=1)

    both = cg[...].reshape(256, 1024)

    def x_slice(f):
        return pl.ds(pl.multiple_of((f // 2) * 288, 32), 288)

    def kernel_chunk(a, value):
        for t in range(9):
            kgb[a, t * 128 : (t + 1) * 128] = value[:, t * 128 : (t + 1) * 128].astype(BF16)
        return [send(kgb.at[a, x_slice(f)], kgr.at[a, fx], ch, f) for f in fxs]

    kgf[...] = dot(both, window_row(1), NN)
    ks = [kernel_chunk(0, kgf[128:] + dot(cg[0], window_row(0), NN))]
    s2.append(second(1))
    v2 = dot(both, window_row(2), NN)
    ks.append(kernel_chunk(1, kgf[:128] + v2[128:]))
    ks.append(kernel_chunk(2, v2[:128] + dot(cg[1], window_row(3), NN)))

    @pl.loop(0, 8)
    def _(j):
        h = jnp.concatenate([hbuf[0], hbuf[1]], axis=0)
        v = dot(obuf[j].reshape(256, 1024), h, NT)
        lo, hi = v[:, :128], v[:, 128:]
        wgf[j] = jnp.where(co == 0, lo, hi)
        wgs[j] = jnp.where(co == 0, hi, lo).astype(BF16)

    wg_x = send(wgs, wgr, sib)

    def kernel_pair(a):
        total = kgb[a, x_slice(fi)].astype(F32)
        for c in ks[a]:
            c.wait_recv()
        for f in fxs:
            total = total + kgr[a, f // 2].astype(F32)
        kgs[a] = total.astype(BF16)
        return send(kgs.at[a], kgy.at[a], ch, fy)

    ky = [kernel_pair(0)]
    spread(c3t, 1, cgt.at[0], False, one)
    spread(c3t, 2, cgt.at[1], False, one)

    for j, (a0, a1) in enumerate(((1, 2), (0, 1))):
        rows = slice(j * 1152, (j + 1) * 1152)
        kback[rows, 0:128] = k_ref[9 * a0 : 9 * a0 + 9].reshape(1152, 128)
        kback[rows, 128:256] = k_ref[9 * a1 : 9 * a1 + 9].reshape(1152, 128)
    back = (2, 1, 0)

    @pl.loop(0, 4)
    def _(i):
        cols = pl.ds(pl.multiple_of(i * 256, 256), 256)
        wins = windows(c3t, 1, i, back) + windows(c3t, 2, i, back)
        v = dot(jnp.concatenate(wins, axis=1), kback[...], NN)
        ghb[0, :, cols] = v[:, :128].T
        ghb[1, :, cols] = v[:, 128:].T

    ky.append(kernel_pair(1))
    ky.append(kernel_pair(2))
    wg_x.wait_recv()
    wgf[...] = wgf[...] + wgr[...].astype(F32)
    wgp[...] = wgf[...].astype(BF16)

    def f_pair(f):
        return pl.ds((f // 2) * 2, 2)

    wq = [send(wgp.at[f_pair(f)], wgq.at[fx], ch, f) for f in fxs]

    for c in s2[0]:
        c.wait_recv()
    pbuf[here[0]] = (
        pbuf[here[0]].astype(F32) + r2[0, 0].astype(F32) + r2[1, 0].astype(F32)
    ).astype(BF16)
    s3 = send(pbuf.at[here[0]], r3, yn)

    kq = []
    for a in range(3):
        ky[a].wait_recv()
        kgall[a, x_slice(fi)] = (kgs[a].astype(F32) + kgy[a].astype(F32)).astype(BF16)
        kq += [
            send(kgall.at[a, x_slice(fi)], kgall.at[a, x_slice(fi)], ch, f) for f in fxs
        ]

    g_up.wait_recv()
    g_dn.wait_recv()
    spread(c3t, 0, chalo.at[0], False, first)
    spread(c3t, 3, chalo.at[1], False, last)

    for plane in range(2):
        @pl.loop(0, 4)
        def _(i):
            cols = pl.ds(pl.multiple_of(i * 256, 256), 256)
            wins = windows(c3t, 3 * plane, i, back)
            taps = k_ref[18 * (1 - plane) : 18 * (1 - plane) + 9].reshape(1152, 128)
            v = dot(jnp.concatenate(wins, axis=1), taps, NN)
            ig_out[plane, :, cols] = (ghb[plane, :, cols] + v.T).astype(BF16)

    total = wgf[f_pair(fi)]
    for c in wq:
        c.wait_recv()
    for f in fxs:
        total = total + wgq[f // 2].astype(F32)
    wgf[f_pair(fi)] = total
    wgy[...] = wgf[fy].astype(BF16)
    wy = send(wgy, wgz, ch, fy)

    for c in s2[1]:
        c.wait_recv()
    s3.wait_recv()
    for half in range(2):
        p4[half] = (
            pbuf[here[1], half].astype(F32) + r2[0, 1, half].astype(F32)
            + r2[1, 1, half].astype(F32) + r3[half].astype(F32)
        ).astype(BF16)
    s4 = send(p4.at[oth], r4, sib)
    p_out[own] = p4[own]
    wy.wait_recv()
    wg_out[...] = wgf[fi] + wgz[...].astype(F32)
    for c in kq:
        c.wait_recv()
    for a in range(3):
        kg_out[9 * a : 9 * a + 9] = kgall[a].astype(F32).reshape(9, 128, 128)
    s4.wait_recv()
    p_out[oth] = r4[...]
    for c in sent:
        c.wait_send()


def body(inputs, conv_kernel, proj_weight, out_grad):
    x = inputs.transpose(1, 2, 0)
    o = out_grad.transpose(1, 0, 2)
    vmem = pl.BlockSpec(memory_space=pltpu.VMEM)
    shapes = [
        ((8, 2, 128, 1024), BF16),
        ((2, 1024, 128), BF16),
        ((4, 1088, 384), BF16),
        ((256, 3456), BF16),
        ((2, 2048, 128), BF16),
        ((256, 2048), BF16),
        ((2, 128, 1024), BF16),
        ((2, 128, 1024), BF16),
        ((2, 128, 1024), F32),
        ((8, 2, 128, 1024), BF16),
        ((2, 2, 128, 1024), BF16),
        ((2, 2, 2, 128, 1024), BF16),
        ((2, 128, 1024), BF16),
        ((2, 128, 1024), BF16),
        ((128, 1024), BF16),
        ((2, 128, 1024), F32),
        ((128, 1024), BF16),
        ((128, 1024), BF16),
        ((2, 128, 1024), BF16),
        ((2, 1024, 128), BF16),
        ((2, 1024, 128), BF16),
        ((4, 1088, 384), BF16),
        ((2304, 256), BF16),
        ((8, 256, 128), F32),
        ((8, 256, 128), BF16),
        ((8, 256, 128), BF16),
        ((8, 256, 128), BF16),
        ((4, 2, 256, 128), BF16),
        ((256, 128), BF16),
        ((256, 128), BF16),
        ((256, 1152), F32),
        ((3, 1152, 128), BF16),
        ((3, 4, 288, 128), BF16),
        ((3, 288, 128), BF16),
        ((3, 288, 128), BF16),
        ((3, 1152, 128), BF16),
    ]
    projected, input_grad, kernel_grad, weight_grad = pl.pallas_call(
        kernel,
        out_shape=(
            jax.ShapeDtypeStruct((2, 128, 1024), BF16),
            jax.ShapeDtypeStruct((2, 128, 1024), BF16),
            jax.ShapeDtypeStruct((27, 128, 128), F32),
            jax.ShapeDtypeStruct((256, 128), F32),
        ),
        in_specs=[vmem] * 4,
        out_specs=(vmem,) * 4,
        scratch_shapes=[pltpu.VMEM(s, d) for s, d in shapes]
        + [pltpu.SemaphoreType.DMA((N_SEMS,)), pltpu.SemaphoreType.DMA((N_SEMS,))],
        compiler_params=pltpu.CompilerParams(
            collective_id=0, has_side_effects=True, vmem_limit_bytes=56 * 1024 * 1024
        ),
    )(x, conv_kernel, proj_weight, o)
    return (
        projected.transpose(1, 0, 2), input_grad.transpose(1, 0, 2), kernel_grad, weight_grad
    )


def solution(mesh):
    in_specs = (
        P("chan", "filt", None),
        P(None, "chan", None),
        P("filt", "chan"),
        P("chan", "filt", None),
    )
    out_specs = (
        P("chan", "filt", None),
        P("chan", "filt", None),
        P(None, "chan", None),
        P("filt", "chan"),
    )
    return jax.shard_map(body, mesh=mesh, in_specs=in_specs, out_specs=out_specs, check_vma=False)
```

```python
import jax
import jax.numpy as jnp
from jax import lax
from jax.experimental import pallas as pl
from jax.experimental.pallas import tpu as pltpu
from jax.sharding import PartitionSpec as P

MESH = pl.DeviceIdType.MESH
F32 = jnp.float32
BF16 = jnp.bfloat16
NN = (((1,), (0,)), ((), ()))
NT = (((1,), (1,)), ((), ()))
N_SEMS = 128


def dot(a, b, dims):
    return lax.dot_general(a, b, dims, preferred_element_type=F32)


def kernel(
    x_in, k_in, w_in_ref, o_in,
    p_res, ig_res, kg_res, wg_res,
    x_raw, k_ref, w_ref, o_raw, x_ref, o_ref,
    p_out, ig_out, kg_out, wg_out,
    obuf, xhalo, x3t, k3, wbuf, wt, hown, hbuf, der,
    pbuf, sbuf, r1, r2, r3,
    ghb, ghs, ghr, cg, cgt, chalo, c3t, kback,
    wgf, wgs, wgr, wgp, wgq, wgy, wgz,
    kgf, kgb, kgr, kgs, kgy, kgall,
    ssem, rsem, lsem,
):
    ch = lax.axis_index("chan")
    fi = lax.axis_index("filt")
    co = ch % 2
    q = ch // 2
    yl = q % 2
    z = q // 2
    sib = ch + 1 - 2 * co
    zp = (ch + 4) % 16
    zm = (ch + 12) % 16
    yn = ch + 2 - 4 * yl
    own, oth = co, 1 - co
    flip = 1 - 2 * yl
    q_zp = ((z + 1) % 4) * 2 + yl
    q_zm = ((z + 3) % 4) * 2 + yl
    q_z2 = ((z + 2) % 4) * 2 + yl
    fx = fi // 2
    fy = fi + 1 - 2 * (fi % 2)
    f_up, f_dn = (fi + 1) % 8, (fi + 7) % 8
    fxs = [(fi + 2 * d) % 8 for d in range(1, 4)]
    sent = []

    def send(src, dst, chan_id, filt_id=None):
        i = len(sent)
        copy = pltpu.make_async_remote_copy(
            src_ref=src, dst_ref=dst, send_sem=ssem.at[i], recv_sem=rsem.at[i],
            device_id=(chan_id, fi if filt_id is None else filt_id), device_id_type=MESH,
        )
        copy.start()
        sent.append(copy)
        return copy

    def pass_on(ref, chan_id):
        return send(ref, ref, chan_id)

    def local(src, dst, i):
        copy = pltpu.make_async_copy(src, dst, lsem.at[i])
        copy.start()
        return copy

    o_load = local(o_in, o_raw, 0)
    w_load = local(w_in_ref, w_ref, 1)
    x_load = local(x_in, x_raw, 2)
    k_load = local(k_in, k_ref, 3)

    barrier = pltpu.get_barrier_semaphore()
    for c in (sib, zp, zm, yn):
        pl.semaphore_signal(barrier, inc=1, device_id=(c, fi), device_id_type=MESH)
    for f in [f_up, f_dn] + fxs:
        pl.semaphore_signal(barrier, inc=1, device_id=(ch, f), device_id_type=MESH)
    o_load.wait()
    for plane in range(2):
        o_ref[plane] = o_raw[:, plane]
    w_load.wait()
    pl.semaphore_wait(barrier, 9)

    c1 = send(o_ref.at[oth], obuf.at[q, own], sib)
    a_p = send(o_ref.at[own], obuf.at[q, own], zp)
    a_m = send(o_ref.at[own], obuf.at[q, own], zm)
    a_y = send(o_ref.at[own], obuf.at[q, own], yn)

    def block_of(f):
        return pl.ds(pl.multiple_of(f * 256, 256), 256)

    w_y = send(w_ref, wbuf.at[own, block_of(fi)], ch, fy)
    w_in = [send(w_ref, wbuf.at[own, block_of(fi)], ch, f) for f in fxs]

    wbuf[own, block_of(fi)] = w_ref[...]
    obuf[q, own] = o_ref[own]
    x_load.wait()
    for plane in range(2):
        @pl.loop(0, 4)
        def _(i):
            cols = pl.ds(pl.multiple_of(i * 256, 256), 256)
            x_ref[plane, cols] = x_raw[:, plane, cols].astype(F32).T.astype(BF16)

    c1.wait_recv()
    b_y = pass_on(obuf.at[q, oth], yn)
    b_p = pass_on(obuf.at[q, oth], zp)
    b_m = pass_on(obuf.at[q, oth], zm)

    k_load.wait()
    for t in range(27):
        a, lane = t // 9, (t % 9) * 128
        tap = k_ref[t]
        if a > 0:
            k3[0:128, (a - 1) * 1152 + lane : (a - 1) * 1152 + lane + 128] = tap
        if a < 2:
            k3[128:256, a * 1152 + lane : a * 1152 + lane + 128] = tap
        if a == 0:
            k3[0:128, 2304 + lane : 2304 + lane + 128] = tap
        if a == 2:
            k3[128:256, 2304 + lane : 2304 + lane + 128] = tap

    def spread(dst, at, src, low, keep):
        edge = jnp.zeros((32, 384), BF16)
        dst[at, 0:32] = edge
        dst[at, 1056:1088] = edge

        @pl.loop(0, 4)
        def _(i):
            rows = pl.ds(pl.multiple_of(i * 256, 256), 256)
            v = src[rows].astype(F32) * keep
            r = lax.broadcasted_iota(jnp.int32, (256, 128), 0) % 32
            prev = jnp.where(r == 0, 0.0, pltpu.roll(v, 1, 0))
            after = jnp.where(r == 31, 0.0, pltpu.roll(v, 255, 0))
            left, right = (prev, after) if low else (after, prev)
            to = pl.ds(pl.multiple_of(i * 256 + 32, 32), 256)
            dst[at, to, 0:128] = left.astype(BF16)
            dst[at, to, 128:256] = v.astype(BF16)
            dst[at, to, 256:384] = right.astype(BF16)

    one = jnp.float32(1.0)
    first = jnp.where(fi == 0, 0.0, 1.0).astype(F32)
    last = jnp.where(fi == 7, 0.0, 1.0).astype(F32)
    spread(x3t, 1, x_ref.at[0], True, one)
    spread(x3t, 2, x_ref.at[1], True, one)

    lower, upper = pl.ds(0, 64), pl.ds(64, 64)
    a_y.wait_recv()
    ya_p = pass_on(obuf.at[q + flip, own, upper], zp)
    ya_m = pass_on(obuf.at[q + flip, own, upper], zm)
    x_up = send(x_ref.at[1], xhalo.at[0], ch, f_up)
    x_dn = send(x_ref.at[0], xhalo.at[1], ch, f_dn)
    w_y.wait_recv()
    w_in += [
        send(wbuf.at[own, block_of(fy)], wbuf.at[own, block_of(fy)], ch, f) for f in fxs
    ]
    a_p.wait_recv()
    forwards = [pass_on(obuf.at[q_zm, own, lower], zp)]
    across = [pass_on(obuf.at[q_zm, own, lower], yn)]
    a_m.wait_recv()
    forwards.append(pass_on(obuf.at[q_zp, own, upper], zm))
    across.append(pass_on(obuf.at[q_zp, own, lower], yn))

    def windows(src, plane, i, order):
        return [
            src[plane, pl.ds(pl.multiple_of(i * 256 + 32 * b, 32), 256)] for b in order
        ]

    def convolve(start, stop):
        @pl.loop(start, stop)
        def _(i):
            cols = pl.ds(pl.multiple_of(i * 256, 256), 256)
            wins = windows(x3t, 1, i, range(3)) + windows(x3t, 2, i, range(3))
            v = dot(k3[:, 0:2304], jnp.concatenate(wins, axis=1), NT)
            der[0, :, cols] = v[:128]
            der[1, :, cols] = v[128:]

    def activate(plane):
        @pl.loop(0, 4)
        def _(i):
            cols = pl.ds(pl.multiple_of(i * 256, 256), 256)
            wins = windows(x3t, 3 * plane, i, range(3))
            taps = k3[pl.ds(pl.multiple_of(plane * 128, 128), 128), 2304:3456]
            v = der[plane, :, cols] + dot(taps, jnp.concatenate(wins, axis=1), NT)
            s = 0.7978845608028654
            sq = v * v
            t = jnp.tanh(s * (v + 0.044715 * sq * v))
            hown[plane, :, cols] = (0.5 * v * (1.0 + t)).astype(BF16)
            der[plane, :, cols] = 0.5 * (1.0 + t) + 0.5 * v * (1.0 - t * t) * (
                s * (1.0 + 3 * 0.044715 * sq)
            )

    convolve(0, 2)
    b_y.wait_recv()
    yb_p = pass_on(obuf.at[q + flip, oth], zp)
    yb_m = pass_on(obuf.at[q + flip, oth], zm)
    b_p.wait_recv()
    forwards.append(pass_on(obuf.at[q_zm, oth, lower], zp))
    b_m.wait_recv()
    forwards.append(pass_on(obuf.at[q_zp, oth, upper], zm))
    convolve(2, 4)
    forwards[0].wait_recv()
    across.append(pass_on(obuf.at[q_z2, own, lower], yn))
    for c in w_in:
        c.wait_recv()
    w_sib = send(wbuf.at[own], wbuf.at[own], sib)

    x_up.wait_recv()
    x_dn.wait_recv()
    spread(x3t, 0, xhalo.at[0], True, first)
    spread(x3t, 3, xhalo.at[1], True, last)
    activate(oth)
    h_x = send(hown.at[oth], hbuf.at[own], sib)
    ya_p.wait_recv()
    forwards.append(pass_on(obuf.at[q_zm + flip, own, pl.ds(64, 32)], zp))
    ya_m.wait_recv()
    forwards.append(pass_on(obuf.at[q_zp + flip, own, pl.ds(96, 32)], zm))
    activate(own)
    hbuf[own] = hown[own]

    w_sib.wait_recv()

    @pl.loop(0, 8)
    def _(j):
        rows = block_of(j)
        for half in range(2):
            block = wbuf[half, rows].astype(F32)
            wt[half * 128 : (half + 1) * 128, rows] = block.T.astype(BF16)

    yb_p.wait_recv()
    forwards.append(pass_on(obuf.at[q_zm + flip, oth, lower], zp))
    yb_m.wait_recv()
    forwards.append(pass_on(obuf.at[q_zp + flip, oth, upper], zm))
    h_x.wait_recv()

    def project(at):
        rows = block_of(at)
        w = jnp.concatenate([wbuf[0, rows], wbuf[1, rows]], axis=1)

        @pl.loop(0, 4)
        def _(i):
            cols = pl.ds(pl.multiple_of(i * 256, 256), 256)
            h = jnp.concatenate([hbuf[0, :, cols], hbuf[1, :, cols]], axis=0)
            v = dot(w, h, NN)
            lo, hi = v[:128], v[128:]
            pbuf[at, own, :, cols] = jnp.where(co == 0, lo, hi).astype(BF16)
            sbuf[at, :, cols] = jnp.where(co == 0, hi, lo).astype(BF16)

        return send(sbuf.at[at], pbuf.at[at, own], sib)

    far = (q_z2 + flip, q_z2)
    up = (q_zp + flip, q_zp)
    down = (q_zm + flip, q_zm)
    here = (q + flip, q)
    ph_far = [project(at) for at in far]
    ph_near = [project(up[0]), project(down[0])]
    s1 = []
    for i in range(2):
        ph_far[i].wait_recv()
        s1.append((
            send(pbuf.at[far[i], 0], r1.at[0, i], zp), send(pbuf.at[far[i], 1], r1.at[1, i], zm)
        ))
    ph_near += [project(at) for at in (up[1], down[1]) + here]
    for c in forwards[1:] + across:
        c.wait_recv()

    @pl.loop(0, 4)
    def _(i):
        cols = pl.ds(pl.multiple_of(i * 256, 256), 256)
        o = obuf[:, :, :, cols].reshape(2048, 256)
        v = dot(wt[...], o, NN)
        ghb[0, :, cols] = v[:128]
        ghb[1, :, cols] = v[128:]

    ghs[...] = ghb[oth].astype(BF16)
    g_x = send(ghs, ghr, sib)

    def to_grad(plane, source):
        @pl.loop(0, 4)
        def _(i):
            cols = pl.ds(pl.multiple_of(i * 256, 256), 256)
            v = (source[:, cols].astype(F32) * der[plane, :, cols]).astype(BF16)
            cg[plane, :, cols] = v
            cgt[plane, cols] = v.astype(F32).T.astype(BF16)

    to_grad(own, ghb.at[own])
    g_x.wait_recv()
    to_grad(oth, ghr)
    g_up = send(cgt.at[1], chalo.at[0], ch, f_up)
    g_dn = send(cgt.at[0], chalo.at[1], ch, f_dn)

    for c in ph_near:
        c.wait_recv()

    def second(i):
        for side, block in ((0, up[i]), (1, down[i])):
            s1[i][side].wait_recv()
            pbuf[block, side] = (
                pbuf[block, side].astype(F32) + r1[side, i].astype(F32)
            ).astype(BF16)
        return (
            send(pbuf.at[up[i]], r2.at[0, i], zp), send(pbuf.at[down[i]], r2.at[1, i], zm)
        )

    s2 = [second(0)]

    def window_row(plane):
        return jnp.concatenate([x3t[plane, 32 * b : 32 * b + 1024] for b in range(3)], axis=1)

    both = cg[...].reshape(256, 1024)

    def x_slice(f):
        return pl.ds(pl.multiple_of((f // 2) * 288, 32), 288)

    def kernel_chunk(a, value):
        for t in range(9):
            kgb[a, t * 128 : (t + 1) * 128] = value[:, t * 128 : (t + 1) * 128].astype(BF16)
        return [send(kgb.at[a, x_slice(f)], kgr.at[a, fx], ch, f) for f in fxs]

    kgf[...] = dot(both, window_row(1), NN)
    ks = [kernel_chunk(0, kgf[128:] + dot(cg[0], window_row(0), NN))]
    v2 = dot(both, window_row(2), NN)
    ks.append(kernel_chunk(1, kgf[:128] + v2[128:]))
    ks.append(kernel_chunk(2, v2[:128] + dot(cg[1], window_row(3), NN)))

    @pl.loop(0, 8)
    def _(j):
        h = jnp.concatenate([hbuf[0], hbuf[1]], axis=0)
        v = dot(obuf[j].reshape(256, 1024), h, NT)
        lo, hi = v[:, :128], v[:, 128:]
        wgf[j] = jnp.where(co == 0, lo, hi)
        wgs[j] = jnp.where(co == 0, hi, lo).astype(BF16)

    wg_x = send(wgs, wgr, sib)

    def kernel_pair(a):
        total = kgb[a, x_slice(fi)].astype(F32)
        for c in ks[a]:
            c.wait_recv()
        for f in fxs:
            total = total + kgr[a, f // 2].astype(F32)
        kgs[a] = total.astype(BF16)
        return send(kgs.at[a], kgy.at[a], ch, fy)

    ky = [kernel_pair(0)]
    spread(c3t, 1, cgt.at[0], False, one)
    spread(c3t, 2, cgt.at[1], False, one)

    for j, (a0, a1) in enumerate(((1, 2), (0, 1))):
        rows = slice(j * 1152, (j + 1) * 1152)
        kback[rows, 0:128] = k_ref[9 * a0 : 9 * a0 + 9].reshape(1152, 128)
        kback[rows, 128:256] = k_ref[9 * a1 : 9 * a1 + 9].reshape(1152, 128)
    back = (2, 1, 0)

    @pl.loop(0, 4)
    def _(i):
        cols = pl.ds(pl.multiple_of(i * 256, 256), 256)
        wins = windows(c3t, 1, i, back) + windows(c3t, 2, i, back)
        v = dot(jnp.concatenate(wins, axis=1), kback[...], NN)
        ghb[0, :, cols] = v[:, :128].T
        ghb[1, :, cols] = v[:, 128:].T

    ky.append(kernel_pair(1))
    ky.append(kernel_pair(2))
    wg_x.wait_recv()
    wgf[...] = wgf[...] + wgr[...].astype(F32)
    wgp[...] = wgf[...].astype(BF16)

    def f_pair(f):
        return pl.ds((f // 2) * 2, 2)

    wq = [send(wgp.at[f_pair(f)], wgq.at[fx], ch, f) for f in fxs]

    for c in s2[0]:
        c.wait_recv()
    pbuf[here[0]] = (
        pbuf[here[0]].astype(F32) + r2[0, 0].astype(F32) + r2[1, 0].astype(F32)
    ).astype(BF16)
    s3 = send(pbuf.at[here[0]], r3, yn)
    s2.append(second(1))

    kq = []
    for a in range(3):
        ky[a].wait_recv()
        kgall[a, x_slice(fi)] = (kgs[a].astype(F32) + kgy[a].astype(F32)).astype(BF16)
        kq += [
            send(kgall.at[a, x_slice(fi)], kgall.at[a, x_slice(fi)], ch, f) for f in fxs
        ]

    g_up.wait_recv()
    g_dn.wait_recv()
    spread(c3t, 0, chalo.at[0], False, first)
    spread(c3t, 3, chalo.at[1], False, last)

    for plane in range(2):
        @pl.loop(0, 4)
        def _(i):
            cols = pl.ds(pl.multiple_of(i * 256, 256), 256)
            wins = windows(c3t, 3 * plane, i, back)
            taps = k_ref[18 * (1 - plane) : 18 * (1 - plane) + 9].reshape(1152, 128)
            v = dot(jnp.concatenate(wins, axis=1), taps, NN)
            ig_out[:, plane, cols] = (ghb[plane, :, cols] + v.T).astype(BF16)

    ig_store = local(ig_out, ig_res, 4)
    total = wgf[f_pair(fi)]
    for c in wq:
        c.wait_recv()
    for f in fxs:
        total = total + wgq[f // 2].astype(F32)
    wgf[f_pair(fi)] = total
    wgy[...] = wgf[fy].astype(BF16)
    wy = send(wgy, wgz, ch, fy)

    wy.wait_recv()
    wg_out[...] = wgf[fi] + wgz[...].astype(F32)
    stores = [ig_store, local(wg_out, wg_res, 5)]
    for a in range(3):
        for c in kq[3 * a : 3 * a + 3]:
            c.wait_recv()
        kg_out[9 * a : 9 * a + 9] = kgall[a].astype(F32).reshape(9, 128, 128)
        part = pl.ds(9 * a, 9)
        stores.append(local(kg_out.at[part], kg_res.at[part], 6 + a))
    for c in s2[1]:
        c.wait_recv()
    s3.wait_recv()
    for plane in range(2):
        p_out[:, plane] = (
            pbuf[here[1], plane].astype(F32) + r2[0, 1, plane].astype(F32)
            + r2[1, 1, plane].astype(F32) + r3[plane].astype(F32)
        ).astype(BF16)
    stores.append(local(p_out, p_res, 9))
    for c in stores:
        c.wait()
    for c in sent:
        c.wait_send()


def body(inputs, conv_kernel, proj_weight, out_grad):
    anywhere = pl.BlockSpec(memory_space=pl.ANY)
    shapes = [
        ((128, 2, 1024), BF16),
        ((27, 128, 128), BF16),
        ((256, 128), BF16),
        ((128, 2, 1024), BF16),
        ((2, 1024, 128), BF16),
        ((2, 128, 1024), BF16),
        ((128, 2, 1024), BF16),
        ((128, 2, 1024), BF16),
        ((27, 128, 128), F32),
        ((256, 128), F32),
        ((8, 2, 128, 1024), BF16),
        ((2, 1024, 128), BF16),
        ((4, 1088, 384), BF16),
        ((256, 3456), BF16),
        ((2, 2048, 128), BF16),
        ((256, 2048), BF16),
        ((2, 128, 1024), BF16),
        ((2, 128, 1024), BF16),
        ((2, 128, 1024), F32),
        ((8, 2, 128, 1024), BF16),
        ((8, 128, 1024), BF16),
        ((2, 2, 128, 1024), BF16),
        ((2, 2, 2, 128, 1024), BF16),
        ((2, 128, 1024), BF16),
        ((2, 128, 1024), F32),
        ((128, 1024), BF16),
        ((128, 1024), BF16),
        ((2, 128, 1024), BF16),
        ((2, 1024, 128), BF16),
        ((2, 1024, 128), BF16),
        ((4, 1088, 384), BF16),
        ((2304, 256), BF16),
        ((8, 256, 128), F32),
        ((8, 256, 128), BF16),
        ((8, 256, 128), BF16),
        ((8, 256, 128), BF16),
        ((4, 2, 256, 128), BF16),
        ((256, 128), BF16),
        ((256, 128), BF16),
        ((256, 1152), F32),
        ((3, 1152, 128), BF16),
        ((3, 4, 288, 128), BF16),
        ((3, 288, 128), BF16),
        ((3, 288, 128), BF16),
        ((3, 1152, 128), BF16),
    ]
    return pl.pallas_call(
        kernel,
        out_shape=(
            jax.ShapeDtypeStruct((128, 2, 1024), BF16),
            jax.ShapeDtypeStruct((128, 2, 1024), BF16),
            jax.ShapeDtypeStruct((27, 128, 128), F32),
            jax.ShapeDtypeStruct((256, 128), F32),
        ),
        in_specs=[anywhere] * 4,
        out_specs=(anywhere,) * 4,
        scratch_shapes=[pltpu.VMEM(s, d) for s, d in shapes]
        + [pltpu.SemaphoreType.DMA((N_SEMS,)), pltpu.SemaphoreType.DMA((N_SEMS,)), pltpu.SemaphoreType.DMA((10,))],
        compiler_params=pltpu.CompilerParams(
            collective_id=0, has_side_effects=True, vmem_limit_bytes=56 * 1024 * 1024
        ),
    )(inputs, conv_kernel, proj_weight, out_grad)


def solution(mesh):
    in_specs = (
        P("chan", "filt", None),
        P(None, "chan", None),
        P("filt", "chan"),
        P("chan", "filt", None),
    )
    out_specs = (
        P("chan", "filt", None),
        P("chan", "filt", None),
        P(None, "chan", None),
        P("filt", "chan"),
    )
    return jax.shard_map(body, mesh=mesh, in_specs=in_specs, out_specs=out_specs, check_vma=False)
```

```python
import jax
import jax.numpy as jnp
from jax import lax
from jax.experimental import pallas as pl
from jax.experimental.pallas import tpu as pltpu
from jax.sharding import PartitionSpec as P

MESH = pl.DeviceIdType.MESH
F32 = jnp.float32
BF16 = jnp.bfloat16
NN = (((1,), (0,)), ((), ()))
NT = (((1,), (1,)), ((), ()))
N_SEMS = 128
PIECES = (2, 2, 3, 1)


def dot(a, b, dims):
    return lax.dot_general(a, b, dims, preferred_element_type=F32)


def kernel(
    x_in, k_in, w_in_ref, o_in,
    p_res, ig_res, kg_res, wg_res,
    x_raw, k_ref, w_ref, o_raw, x_ref, o_ref,
    p_out, ig_out, kg_out, wg_out,
    obuf, xhalo, x3t, k3, wbuf, wt, hown, hbuf, der,
    pbuf, sbuf, r1, r2, r3,
    ghb, ghs, ghr, cg, cgt, chalo, c3t, kback,
    wgf, wgs, wgr, wgp, wgq, wgy, wgz,
    kgf, kgb, kgr, kgs, kgy, kgall,
    ssem, rsem, lsem,
):
    ch = lax.axis_index("chan")
    fi = lax.axis_index("filt")
    co = ch % 2
    q = ch // 2
    yl = q % 2
    z = q // 2
    sib = ch + 1 - 2 * co
    zp = (ch + 4) % 16
    zm = (ch + 12) % 16
    yn = ch + 2 - 4 * yl
    own, oth = co, 1 - co
    flip = 1 - 2 * yl
    q_zp = ((z + 1) % 4) * 2 + yl
    q_zm = ((z + 3) % 4) * 2 + yl
    q_z2 = ((z + 2) % 4) * 2 + yl
    fx = fi // 2
    fy = fi + 1 - 2 * (fi % 2)
    f_up, f_dn = (fi + 1) % 8, (fi + 7) % 8
    fxs = [(fi + 2 * d) % 8 for d in range(1, 4)]
    sent = []

    def send(src, dst, chan_id, filt_id=None):
        i = len(sent)
        copy = pltpu.make_async_remote_copy(
            src_ref=src, dst_ref=dst, send_sem=ssem.at[i], recv_sem=rsem.at[i],
            device_id=(chan_id, fi if filt_id is None else filt_id), device_id_type=MESH,
        )
        copy.start()
        sent.append(copy)
        return copy

    def pass_on(ref, chan_id):
        return send(ref, ref, chan_id)

    def local(src, dst, i):
        copy = pltpu.make_async_copy(src, dst, lsem.at[i])
        copy.start()
        return copy

    o_load = local(o_in, o_raw, 0)
    w_load = local(w_in_ref, w_ref, 1)
    x_load = local(x_in, x_raw, 2)
    k_load = local(k_in, k_ref, 3)

    barrier = pltpu.get_barrier_semaphore()
    for c in (sib, zp, zm, yn):
        pl.semaphore_signal(barrier, inc=1, device_id=(c, fi), device_id_type=MESH)
    for f in [f_up, f_dn] + fxs:
        pl.semaphore_signal(barrier, inc=1, device_id=(ch, f), device_id_type=MESH)
    o_load.wait()
    for plane in range(2):
        o_ref[plane] = o_raw[:, plane]
    w_load.wait()
    pl.semaphore_wait(barrier, 9)

    c1 = send(o_ref.at[oth], obuf.at[q, own], sib)
    a_p = send(o_ref.at[own], obuf.at[q, own], zp)
    a_m = send(o_ref.at[own], obuf.at[q, own], zm)
    a_y = send(o_ref.at[own], obuf.at[q, own], yn)

    def block_of(f):
        return pl.ds(pl.multiple_of(f * 256, 256), 256)

    w_y = send(w_ref, wbuf.at[own, block_of(fi)], ch, fy)
    w_in = [send(w_ref, wbuf.at[own, block_of(fi)], ch, f) for f in fxs]

    wbuf[own, block_of(fi)] = w_ref[...]
    obuf[q, own] = o_ref[own]
    x_load.wait()
    for plane in range(2):
        @pl.loop(0, 4)
        def _(i):
            cols = pl.ds(pl.multiple_of(i * 256, 256), 256)
            x_ref[plane, cols] = x_raw[:, plane, cols].astype(F32).T.astype(BF16)

    c1.wait_recv()
    b_y = pass_on(obuf.at[q, oth], yn)
    b_p = pass_on(obuf.at[q, oth], zp)
    b_m = pass_on(obuf.at[q, oth], zm)

    k_load.wait()
    for t in range(27):
        a, lane = t // 9, (t % 9) * 128
        tap = k_ref[t]
        if a > 0:
            k3[0:128, (a - 1) * 1152 + lane : (a - 1) * 1152 + lane + 128] = tap
        if a < 2:
            k3[128:256, a * 1152 + lane : a * 1152 + lane + 128] = tap
        if a == 0:
            k3[0:128, 2304 + lane : 2304 + lane + 128] = tap
        if a == 2:
            k3[128:256, 2304 + lane : 2304 + lane + 128] = tap

    def spread(dst, at, src, low, keep):
        edge = jnp.zeros((32, 384), BF16)
        dst[at, 0:32] = edge
        dst[at, 1056:1088] = edge

        @pl.loop(0, 4)
        def _(i):
            rows = pl.ds(pl.multiple_of(i * 256, 256), 256)
            v = src[rows].astype(F32) * keep
            r = lax.broadcasted_iota(jnp.int32, (256, 128), 0) % 32
            prev = jnp.where(r == 0, 0.0, pltpu.roll(v, 1, 0))
            after = jnp.where(r == 31, 0.0, pltpu.roll(v, 255, 0))
            left, right = (prev, after) if low else (after, prev)
            to = pl.ds(pl.multiple_of(i * 256 + 32, 32), 256)
            dst[at, to, 0:128] = left.astype(BF16)
            dst[at, to, 128:256] = v.astype(BF16)
            dst[at, to, 256:384] = right.astype(BF16)

    one = jnp.float32(1.0)
    first = jnp.where(fi == 0, 0.0, 1.0).astype(F32)
    last = jnp.where(fi == 7, 0.0, 1.0).astype(F32)
    spread(x3t, 1, x_ref.at[0], True, one)
    spread(x3t, 2, x_ref.at[1], True, one)

    lower, upper = pl.ds(0, 64), pl.ds(64, 64)
    a_y.wait_recv()
    ya_p = pass_on(obuf.at[q + flip, own, upper], zp)
    ya_m = pass_on(obuf.at[q + flip, own, upper], zm)
    x_up = send(x_ref.at[1], xhalo.at[0], ch, f_up)
    x_dn = send(x_ref.at[0], xhalo.at[1], ch, f_dn)
    w_y.wait_recv()
    w_in += [
        send(wbuf.at[own, block_of(fy)], wbuf.at[own, block_of(fy)], ch, f) for f in fxs
    ]
    a_p.wait_recv()
    forwards = [pass_on(obuf.at[q_zm, own, lower], zp)]
    across = [pass_on(obuf.at[q_zm, own, lower], yn)]
    a_m.wait_recv()
    forwards.append(pass_on(obuf.at[q_zp, own, upper], zm))
    across.append(pass_on(obuf.at[q_zp, own, lower], yn))

    def windows(src, plane, i, order):
        return [
            src[plane, pl.ds(pl.multiple_of(i * 256 + 32 * b, 32), 256)] for b in order
        ]

    def convolve(start, stop):
        @pl.loop(start, stop)
        def _(i):
            cols = pl.ds(pl.multiple_of(i * 256, 256), 256)
            wins = windows(x3t, 1, i, range(3)) + windows(x3t, 2, i, range(3))
            v = dot(k3[:, 0:2304], jnp.concatenate(wins, axis=1), NT)
            der[0, :, cols] = v[:128]
            der[1, :, cols] = v[128:]

    def activate(plane):
        @pl.loop(0, 4)
        def _(i):
            cols = pl.ds(pl.multiple_of(i * 256, 256), 256)
            wins = windows(x3t, 3 * plane, i, range(3))
            taps = k3[pl.ds(pl.multiple_of(plane * 128, 128), 128), 2304:3456]
            v = der[plane, :, cols] + dot(taps, jnp.concatenate(wins, axis=1), NT)
            s = 0.7978845608028654
            sq = v * v
            t = jnp.tanh(s * (v + 0.044715 * sq * v))
            hown[plane, :, cols] = (0.5 * v * (1.0 + t)).astype(BF16)
            der[plane, :, cols] = 0.5 * (1.0 + t) + 0.5 * v * (1.0 - t * t) * (
                s * (1.0 + 3 * 0.044715 * sq)
            )

    convolve(0, 2)
    b_y.wait_recv()
    yb_p = pass_on(obuf.at[q + flip, oth], zp)
    yb_m = pass_on(obuf.at[q + flip, oth], zm)
    b_p.wait_recv()
    forwards.append(pass_on(obuf.at[q_zm, oth, lower], zp))
    b_m.wait_recv()
    forwards.append(pass_on(obuf.at[q_zp, oth, upper], zm))
    convolve(2, 4)
    forwards[0].wait_recv()
    across.append(pass_on(obuf.at[q_z2, own, lower], yn))
    for c in w_in:
        c.wait_recv()
    w_sib = send(wbuf.at[own], wbuf.at[own], sib)

    x_up.wait_recv()
    x_dn.wait_recv()
    spread(x3t, 0, xhalo.at[0], True, first)
    spread(x3t, 3, xhalo.at[1], True, last)
    activate(oth)
    h_x = send(hown.at[oth], hbuf.at[own], sib)
    ya_p.wait_recv()
    forwards.append(pass_on(obuf.at[q_zm + flip, own, pl.ds(64, 32)], zp))
    ya_m.wait_recv()
    forwards.append(pass_on(obuf.at[q_zp + flip, own, pl.ds(96, 32)], zm))
    activate(own)
    hbuf[own] = hown[own]

    w_sib.wait_recv()

    @pl.loop(0, 8)
    def _(j):
        rows = block_of(j)
        for half in range(2):
            block = wbuf[half, rows].astype(F32)
            wt[half * 128 : (half + 1) * 128, rows] = block.T.astype(BF16)

    yb_p.wait_recv()
    forwards.append(pass_on(obuf.at[q_zm + flip, oth, lower], zp))
    yb_m.wait_recv()
    forwards.append(pass_on(obuf.at[q_zp + flip, oth, upper], zm))
    h_x.wait_recv()

    def project(at):
        rows = block_of(at)
        w = jnp.concatenate([wbuf[0, rows], wbuf[1, rows]], axis=1)

        @pl.loop(0, 4)
        def _(i):
            cols = pl.ds(pl.multiple_of(i * 256, 256), 256)
            h = jnp.concatenate([hbuf[0, :, cols], hbuf[1, :, cols]], axis=0)
            v = dot(w, h, NN)
            lo, hi = v[:128], v[128:]
            pbuf[at, own, :, cols] = jnp.where(co == 0, lo, hi).astype(BF16)
            sbuf[at, :, cols] = jnp.where(co == 0, hi, lo).astype(BF16)

        return send(sbuf.at[at], pbuf.at[at, own], sib)

    far = (q_z2 + flip, q_z2)
    up = (q_zp + flip, q_zp)
    down = (q_zm + flip, q_zm)
    here = (q + flip, q)
    ph_far = [project(at) for at in far]
    ph_near = [project(up[0]), project(down[0])]
    s1 = []
    for i in range(2):
        ph_far[i].wait_recv()
        s1.append((
            send(pbuf.at[far[i], 0], r1.at[0, i], zp), send(pbuf.at[far[i], 1], r1.at[1, i], zm)
        ))
    ph_near += [project(at) for at in (up[1], down[1]) + here]
    for c in forwards[1:] + across:
        c.wait_recv()

    @pl.loop(0, 4)
    def _(i):
        cols = pl.ds(pl.multiple_of(i * 256, 256), 256)
        o = obuf[:, :, :, cols].reshape(2048, 256)
        v = dot(wt[...], o, NN)
        ghb[0, :, cols] = v[:128]
        ghb[1, :, cols] = v[128:]

    ghs[...] = ghb[oth].astype(BF16)
    g_x = send(ghs, ghr, sib)

    for c in ph_near:
        c.wait_recv()

    def second(i):
        for side, block in ((0, up[i]), (1, down[i])):
            s1[i][side].wait_recv()
            pbuf[block, side] = (
                pbuf[block, side].astype(F32) + r1[side, i].astype(F32)
            ).astype(BF16)
        return (
            send(pbuf.at[up[i]], r2.at[0, i], zp), send(pbuf.at[down[i]], r2.at[1, i], zm)
        )

    s2 = [second(0)]

    def to_grad(plane, source):
        @pl.loop(0, 4)
        def _(i):
            cols = pl.ds(pl.multiple_of(i * 256, 256), 256)
            v = (source[:, cols].astype(F32) * der[plane, :, cols]).astype(BF16)
            cg[plane, :, cols] = v
            cgt[plane, cols] = v.astype(F32).T.astype(BF16)

    to_grad(own, ghb.at[own])
    g_x.wait_recv()
    to_grad(oth, ghr)
    g_up = send(cgt.at[1], chalo.at[0], ch, f_up)
    g_dn = send(cgt.at[0], chalo.at[1], ch, f_dn)


    def window_row(plane):
        return jnp.concatenate([x3t[plane, 32 * b : 32 * b + 1024] for b in range(3)], axis=1)

    both = cg[...].reshape(256, 1024)

    def x_slice(f):
        return pl.ds(pl.multiple_of((f // 2) * 288, 32), 288)

    def kernel_chunk(a, value):
        for t in range(9):
            kgb[a, t * 128 : (t + 1) * 128] = value[:, t * 128 : (t + 1) * 128].astype(BF16)
        return [send(kgb.at[a, x_slice(f)], kgr.at[a, fx], ch, f) for f in fxs]

    kgf[...] = dot(both, window_row(1), NN)
    ks = [kernel_chunk(0, kgf[128:] + dot(cg[0], window_row(0), NN))]
    v2 = dot(both, window_row(2), NN)
    ks.append(kernel_chunk(1, kgf[:128] + v2[128:]))
    ks.append(kernel_chunk(2, v2[:128] + dot(cg[1], window_row(3), NN)))

    @pl.loop(0, 8)
    def _(j):
        h = jnp.concatenate([hbuf[0], hbuf[1]], axis=0)
        v = dot(obuf[j].reshape(256, 1024), h, NT)
        lo, hi = v[:, :128], v[:, 128:]
        wgf[j] = jnp.where(co == 0, lo, hi)
        wgs[j] = jnp.where(co == 0, hi, lo).astype(BF16)

    wg_x = send(wgs, wgr, sib)

    def kernel_pair(a):
        total = kgb[a, x_slice(fi)].astype(F32)
        for c in ks[a]:
            c.wait_recv()
        for f in fxs:
            total = total + kgr[a, f // 2].astype(F32)
        kgs[a] = total.astype(BF16)
        return send(kgs.at[a], kgy.at[a], ch, fy)

    ky = [kernel_pair(0)]
    spread(c3t, 1, cgt.at[0], False, one)
    spread(c3t, 2, cgt.at[1], False, one)

    for j, (a0, a1) in enumerate(((1, 2), (0, 1))):
        rows = slice(j * 1152, (j + 1) * 1152)
        kback[rows, 0:128] = k_ref[9 * a0 : 9 * a0 + 9].reshape(1152, 128)
        kback[rows, 128:256] = k_ref[9 * a1 : 9 * a1 + 9].reshape(1152, 128)
    back = (2, 1, 0)

    @pl.loop(0, 4)
    def _(i):
        cols = pl.ds(pl.multiple_of(i * 256, 256), 256)
        wins = windows(c3t, 1, i, back) + windows(c3t, 2, i, back)
        v = dot(jnp.concatenate(wins, axis=1), kback[...], NN)
        ghb[0, :, cols] = v[:, :128].T
        ghb[1, :, cols] = v[:, 128:].T

    ky.append(kernel_pair(1))
    ky.append(kernel_pair(2))
    wg_x.wait_recv()
    wgf[...] = wgf[...] + wgr[...].astype(F32)
    wgp[...] = wgf[...].astype(BF16)

    def f_pair(f):
        return pl.ds((f // 2) * 2, 2)

    wq = [send(wgp.at[f_pair(f)], wgq.at[fx], ch, f) for f in fxs]

    s2.append(second(1))
    for c in s2[0]:
        c.wait_recv()
    pbuf[here[0]] = (
        pbuf[here[0]].astype(F32) + r2[0, 0].astype(F32) + r2[1, 0].astype(F32)
    ).astype(BF16)
    s3 = send(pbuf.at[here[0]], r3, yn)

    kq = []
    for a in range(3):
        ky[a].wait_recv()
        kgall[a, x_slice(fi)] = (kgs[a].astype(F32) + kgy[a].astype(F32)).astype(BF16)
        kq += [
            send(kgall.at[a, x_slice(fi)], kgall.at[a, x_slice(fi)], ch, f) for f in fxs
        ]

    g_up.wait_recv()
    g_dn.wait_recv()
    spread(c3t, 0, chalo.at[0], False, first)
    spread(c3t, 3, chalo.at[1], False, last)

    for plane in range(2):
        @pl.loop(0, 4)
        def _(i):
            cols = pl.ds(pl.multiple_of(i * 256, 256), 256)
            wins = windows(c3t, 3 * plane, i, back)
            taps = k_ref[18 * (1 - plane) : 18 * (1 - plane) + 9].reshape(1152, 128)
            v = dot(jnp.concatenate(wins, axis=1), taps, NN)
            ig_out[:, plane, cols] = (ghb[plane, :, cols] + v.T).astype(BF16)

    ig_store = local(ig_out, ig_res, 4)
    total = wgf[f_pair(fi)]
    for c in wq:
        c.wait_recv()
    for f in fxs:
        total = total + wgq[f // 2].astype(F32)
    wgf[f_pair(fi)] = total
    wgy[...] = wgf[fy].astype(BF16)
    wy = send(wgy, wgz, ch, fy)

    wy.wait_recv()
    wg_out[...] = wgf[fi] + wgz[...].astype(F32)
    stores = [ig_store, local(wg_out, wg_res, 5)]
    for a in range(3):
        for c in kq[3 * a : 3 * a + 3]:
            c.wait_recv()
        kg_out[9 * a : 9 * a + 9] = kgall[a].astype(F32).reshape(9, 128, 128)
        part = pl.ds(9 * a, 9)
        stores.append(local(kg_out.at[part], kg_res.at[part], 6 + a))
    for c in s2[1]:
        c.wait_recv()
    s3.wait_recv()
    for plane in range(2):
        p_out[:, plane] = (
            pbuf[here[1], plane].astype(F32) + r2[0, 1, plane].astype(F32)
            + r2[1, 1, plane].astype(F32) + r3[plane].astype(F32)
        ).astype(BF16)
    stores.append(local(p_out, p_res, 9))
    for c in stores:
        c.wait()
    for c in sent:
        c.wait_send()


def copy_kernel(*refs):
    sem = refs[12]
    loads, stores = [], []
    for i in range(4):
        src, held = refs[i], refs[8 + i]
        step = src.shape[0] // PIECES[i]
        for j in range(PIECES[i]):
            part = pl.ds(j * step, step)
            copy = pltpu.make_async_copy(src.at[part], held.at[part], sem.at[0, len(loads)])
            copy.start()
            loads.append((copy, held.at[part], refs[4 + i].at[part]))
    for copy, held, dst in loads:
        copy.wait()
        stores.append(pltpu.make_async_copy(held, dst, sem.at[1, len(stores)]))
        stores[-1].start()
    for copy in stores:
        copy.wait()


def body(inputs, conv_kernel, proj_weight, out_grad):
    anywhere = pl.BlockSpec(memory_space=pl.ANY)
    shapes = [
        ((128, 2, 1024), BF16),
        ((27, 128, 128), BF16),
        ((256, 128), BF16),
        ((128, 2, 1024), BF16),
        ((2, 1024, 128), BF16),
        ((2, 128, 1024), BF16),
        ((128, 2, 1024), BF16),
        ((128, 2, 1024), BF16),
        ((27, 128, 128), F32),
        ((256, 128), F32),
        ((8, 2, 128, 1024), BF16),
        ((2, 1024, 128), BF16),
        ((4, 1088, 384), BF16),
        ((256, 3456), BF16),
        ((2, 2048, 128), BF16),
        ((256, 2048), BF16),
        ((2, 128, 1024), BF16),
        ((2, 128, 1024), BF16),
        ((2, 128, 1024), F32),
        ((8, 2, 128, 1024), BF16),
        ((8, 128, 1024), BF16),
        ((2, 2, 128, 1024), BF16),
        ((2, 2, 2, 128, 1024), BF16),
        ((2, 128, 1024), BF16),
        ((2, 128, 1024), F32),
        ((128, 1024), BF16),
        ((128, 1024), BF16),
        ((2, 128, 1024), BF16),
        ((2, 1024, 128), BF16),
        ((2, 1024, 128), BF16),
        ((4, 1088, 384), BF16),
        ((2304, 256), BF16),
        ((8, 256, 128), F32),
        ((8, 256, 128), BF16),
        ((8, 256, 128), BF16),
        ((8, 256, 128), BF16),
        ((4, 2, 256, 128), BF16),
        ((256, 128), BF16),
        ((256, 128), BF16),
        ((256, 1152), F32),
        ((3, 1152, 128), BF16),
        ((3, 4, 288, 128), BF16),
        ((3, 288, 128), BF16),
        ((3, 288, 128), BF16),
        ((3, 1152, 128), BF16),
    ]
    out_shape = (
        jax.ShapeDtypeStruct((128, 2, 1024), BF16),
        jax.ShapeDtypeStruct((128, 2, 1024), BF16),
        jax.ShapeDtypeStruct((27, 128, 128), F32),
        jax.ShapeDtypeStruct((256, 128), F32),
    )
    results = pl.pallas_call(
        kernel,
        out_shape=out_shape,
        in_specs=[anywhere] * 4,
        out_specs=(anywhere,) * 4,
        scratch_shapes=[pltpu.VMEM(s, d) for s, d in shapes]
        + [pltpu.SemaphoreType.DMA((N_SEMS,)), pltpu.SemaphoreType.DMA((N_SEMS,)), pltpu.SemaphoreType.DMA((10,))],
        compiler_params=pltpu.CompilerParams(
            collective_id=0, has_side_effects=True, vmem_limit_bytes=56 * 1024 * 1024
        ),
    )(inputs, conv_kernel, proj_weight, out_grad)
    return pl.pallas_call(
        copy_kernel,
        out_shape=out_shape,
        in_specs=[anywhere] * 4,
        out_specs=(anywhere,) * 4,
        scratch_shapes=[pltpu.VMEM(o.shape, o.dtype) for o in out_shape]
        + [pltpu.SemaphoreType.DMA((2, sum(PIECES)))],
    )(*results)


def solution(mesh):
    in_specs = (
        P("chan", "filt", None),
        P(None, "chan", None),
        P("filt", "chan"),
        P("chan", "filt", None),
    )
    out_specs = (
        P("chan", "filt", None),
        P("chan", "filt", None),
        P(None, "chan", None),
        P("filt", "chan"),
    )
    return jax.shard_map(body, mesh=mesh, in_specs=in_specs, out_specs=out_specs, check_vma=False)
```

```python
import jax
import jax.numpy as jnp
from jax import lax
from jax.experimental import pallas as pl
from jax.experimental.pallas import tpu as pltpu
from jax.sharding import PartitionSpec as P

MESH = pl.DeviceIdType.MESH
F32 = jnp.float32
BF16 = jnp.bfloat16
NN = (((1,), (0,)), ((), ()))
NT = (((1,), (1,)), ((), ()))
N_SEMS = 128
PIECES = (2, 2, 3, 1)


def dot(a, b, dims):
    return lax.dot_general(a, b, dims, preferred_element_type=F32)


def kernel(
    x_in, k_in, w_in_ref, o_in,
    p_res, ig_res, kg_res, wg_res,
    x_raw, k_ref, w_ref, o_raw, x_ref, o_ref,
    p_out, ig_out, kg_out, wg_out,
    obuf, xhalo, x3t, k3, wbuf, wt, hown, hbuf, der,
    pbuf, sbuf, r1, r2, r3,
    ghb, ghs, ghr, cg, cgt, chalo, c3t, kback,
    wgf, wgs, wgr, wgp, wgq, wgy, wgz,
    kgf, kgb, kgr, kgs, kgy, kgall,
    ssem, rsem, lsem,
):
    ch = lax.axis_index("chan")
    fi = lax.axis_index("filt")
    co = ch % 2
    q = ch // 2
    yl = q % 2
    z = q // 2
    sib = ch + 1 - 2 * co
    zp = (ch + 4) % 16
    zm = (ch + 12) % 16
    yn = ch + 2 - 4 * yl
    own, oth = co, 1 - co
    flip = 1 - 2 * yl
    q_zp = ((z + 1) % 4) * 2 + yl
    q_zm = ((z + 3) % 4) * 2 + yl
    q_z2 = ((z + 2) % 4) * 2 + yl
    fx = fi // 2
    fy = fi + 1 - 2 * (fi % 2)
    f_up, f_dn = (fi + 1) % 8, (fi + 7) % 8
    fxs = [(fi + 2 * d) % 8 for d in range(1, 4)]
    sent = []

    def send(src, dst, chan_id, filt_id=None):
        i = len(sent)
        copy = pltpu.make_async_remote_copy(
            src_ref=src, dst_ref=dst, send_sem=ssem.at[i], recv_sem=rsem.at[i],
            device_id=(chan_id, fi if filt_id is None else filt_id), device_id_type=MESH,
        )
        copy.start()
        sent.append(copy)
        return copy

    def pass_on(ref, chan_id):
        return send(ref, ref, chan_id)

    def local(src, dst, i):
        copy = pltpu.make_async_copy(src, dst, lsem.at[i])
        copy.start()
        return copy

    o_load = local(o_in, o_raw, 0)
    w_load = local(w_in_ref, w_ref, 1)
    x_load = local(x_in, x_raw, 2)
    k_load = local(k_in, k_ref, 3)

    barrier = pltpu.get_barrier_semaphore()
    for c in (sib, zp, zm, yn):
        pl.semaphore_signal(barrier, inc=1, device_id=(c, fi), device_id_type=MESH)
    for f in [f_up, f_dn] + fxs:
        pl.semaphore_signal(barrier, inc=1, device_id=(ch, f), device_id_type=MESH)
    o_load.wait()
    for plane in range(2):
        o_ref[plane] = o_raw[:, plane]
    w_load.wait()
    pl.semaphore_wait(barrier, 9)

    c1 = send(o_ref.at[oth], obuf.at[q, own], sib)
    a_p = send(o_ref.at[own], obuf.at[q, own], zp)
    a_m = send(o_ref.at[own], obuf.at[q, own], zm)
    a_y = send(o_ref.at[own], obuf.at[q, own], yn)

    def block_of(f):
        return pl.ds(pl.multiple_of(f * 256, 256), 256)

    w_y = send(w_ref, wbuf.at[own, block_of(fi)], ch, fy)
    w_in = [send(w_ref, wbuf.at[own, block_of(fi)], ch, f) for f in fxs]

    wbuf[own, block_of(fi)] = w_ref[...]
    obuf[q, own] = o_ref[own]
    x_load.wait()
    for plane in range(2):
        @pl.loop(0, 4)
        def _(i):
            cols = pl.ds(pl.multiple_of(i * 256, 256), 256)
            x_ref[plane, cols] = x_raw[:, plane, cols].astype(F32).T.astype(BF16)

    c1.wait_recv()
    b_y = pass_on(obuf.at[q, oth], yn)
    b_p = pass_on(obuf.at[q, oth], zp)
    b_m = pass_on(obuf.at[q, oth], zm)

    k_load.wait()
    for t in range(27):
        a, lane = t // 9, (t % 9) * 128
        tap = k_ref[t]
        if a > 0:
            k3[0:128, (a - 1) * 1152 + lane : (a - 1) * 1152 + lane + 128] = tap
        if a < 2:
            k3[128:256, a * 1152 + lane : a * 1152 + lane + 128] = tap
        if a == 0:
            k3[0:128, 2304 + lane : 2304 + lane + 128] = tap
        if a == 2:
            k3[128:256, 2304 + lane : 2304 + lane + 128] = tap

    def spread(dst, at, src, low, keep):
        edge = jnp.zeros((32, 384), BF16)
        dst[at, 0:32] = edge
        dst[at, 1056:1088] = edge

        @pl.loop(0, 4)
        def _(i):
            rows = pl.ds(pl.multiple_of(i * 256, 256), 256)
            v = src[rows].astype(F32) * keep
            r = lax.broadcasted_iota(jnp.int32, (256, 128), 0) % 32
            prev = jnp.where(r == 0, 0.0, pltpu.roll(v, 1, 0))
            after = jnp.where(r == 31, 0.0, pltpu.roll(v, 255, 0))
            left, right = (prev, after) if low else (after, prev)
            to = pl.ds(pl.multiple_of(i * 256 + 32, 32), 256)
            dst[at, to, 0:128] = left.astype(BF16)
            dst[at, to, 128:256] = v.astype(BF16)
            dst[at, to, 256:384] = right.astype(BF16)

    one = jnp.float32(1.0)
    first = jnp.where(fi == 0, 0.0, 1.0).astype(F32)
    last = jnp.where(fi == 7, 0.0, 1.0).astype(F32)
    spread(x3t, 1, x_ref.at[0], True, one)
    spread(x3t, 2, x_ref.at[1], True, one)

    lower, upper = pl.ds(0, 64), pl.ds(64, 64)
    a_y.wait_recv()
    ya_p = pass_on(obuf.at[q + flip, own, upper], zp)
    ya_m = pass_on(obuf.at[q + flip, own, upper], zm)
    x_up = send(x_ref.at[1], xhalo.at[0], ch, f_up)
    x_dn = send(x_ref.at[0], xhalo.at[1], ch, f_dn)
    w_y.wait_recv()
    w_in += [
        send(wbuf.at[own, block_of(fy)], wbuf.at[own, block_of(fy)], ch, f) for f in fxs
    ]
    a_p.wait_recv()
    forwards = [pass_on(obuf.at[q_zm, own, lower], zp)]
    across = [pass_on(obuf.at[q_zm, own, lower], yn)]
    a_m.wait_recv()
    forwards.append(pass_on(obuf.at[q_zp, own, upper], zm))
    across.append(pass_on(obuf.at[q_zp, own, lower], yn))

    def windows(src, plane, i, order):
        return [
            src[plane, pl.ds(pl.multiple_of(i * 256 + 32 * b, 32), 256)] for b in order
        ]

    def convolve(start, stop):
        @pl.loop(start, stop)
        def _(i):
            cols = pl.ds(pl.multiple_of(i * 256, 256), 256)
            wins = windows(x3t, 1, i, range(3)) + windows(x3t, 2, i, range(3))
            v = dot(k3[:, 0:2304], jnp.concatenate(wins, axis=1), NT)
            der[0, :, cols] = v[:128]
            der[1, :, cols] = v[128:]

    def activate(plane):
        @pl.loop(0, 4)
        def _(i):
            cols = pl.ds(pl.multiple_of(i * 256, 256), 256)
            wins = windows(x3t, 3 * plane, i, range(3))
            taps = k3[pl.ds(pl.multiple_of(plane * 128, 128), 128), 2304:3456]
            v = der[plane, :, cols] + dot(taps, jnp.concatenate(wins, axis=1), NT)
            s = 0.7978845608028654
            sq = v * v
            t = jnp.tanh(s * (v + 0.044715 * sq * v))
            hown[plane, :, cols] = (0.5 * v * (1.0 + t)).astype(BF16)
            der[plane, :, cols] = 0.5 * (1.0 + t) + 0.5 * v * (1.0 - t * t) * (
                s * (1.0 + 3 * 0.044715 * sq)
            )

    convolve(0, 2)
    b_y.wait_recv()
    yb_p = pass_on(obuf.at[q + flip, oth], zp)
    yb_m = pass_on(obuf.at[q + flip, oth], zm)
    b_p.wait_recv()
    forwards.append(pass_on(obuf.at[q_zm, oth, lower], zp))
    b_m.wait_recv()
    forwards.append(pass_on(obuf.at[q_zp, oth, upper], zm))
    convolve(2, 4)
    forwards[0].wait_recv()
    across.append(pass_on(obuf.at[q_z2, own, lower], yn))
    for c in w_in:
        c.wait_recv()
    w_sib = send(wbuf.at[own], wbuf.at[own], sib)

    x_up.wait_recv()
    x_dn.wait_recv()
    spread(x3t, 0, xhalo.at[0], True, first)
    spread(x3t, 3, xhalo.at[1], True, last)
    activate(oth)
    h_x = send(hown.at[oth], hbuf.at[own], sib)
    ya_p.wait_recv()
    forwards.append(pass_on(obuf.at[q_zm + flip, own, pl.ds(64, 32)], zp))
    ya_m.wait_recv()
    forwards.append(pass_on(obuf.at[q_zp + flip, own, pl.ds(96, 32)], zm))
    activate(own)
    hbuf[own] = hown[own]

    w_sib.wait_recv()

    @pl.loop(0, 8)
    def _(j):
        rows = block_of(j)
        for half in range(2):
            block = wbuf[half, rows].astype(F32)
            wt[half * 128 : (half + 1) * 128, rows] = block.T.astype(BF16)

    yb_p.wait_recv()
    forwards.append(pass_on(obuf.at[q_zm + flip, oth, lower], zp))
    yb_m.wait_recv()
    forwards.append(pass_on(obuf.at[q_zp + flip, oth, upper], zm))
    h_x.wait_recv()

    def project(at):
        rows = block_of(at)
        w = jnp.concatenate([wbuf[0, rows], wbuf[1, rows]], axis=1)

        @pl.loop(0, 4)
        def _(i):
            cols = pl.ds(pl.multiple_of(i * 256, 256), 256)
            h = jnp.concatenate([hbuf[0, :, cols], hbuf[1, :, cols]], axis=0)
            v = dot(w, h, NN)
            lo, hi = v[:128], v[128:]
            pbuf[at, own, :, cols] = jnp.where(co == 0, lo, hi).astype(BF16)
            sbuf[at, :, cols] = jnp.where(co == 0, hi, lo).astype(BF16)

        return send(sbuf.at[at], pbuf.at[at, own], sib)

    far = (q_z2 + flip, q_z2)
    up = (q_zp + flip, q_zp)
    down = (q_zm + flip, q_zm)
    here = (q + flip, q)
    ph_far = [project(at) for at in far]
    ph_near = [project(up[0]), project(down[0])]
    s1 = []
    for i in range(2):
        ph_far[i].wait_recv()
        s1.append((
            send(pbuf.at[far[i], 0], r1.at[0, i], zp), send(pbuf.at[far[i], 1], r1.at[1, i], zm)
        ))
    ph_near += [project(at) for at in (up[1], down[1]) + here]
    for c in forwards[1:] + across:
        c.wait_recv()

    @pl.loop(0, 4)
    def _(i):
        cols = pl.ds(pl.multiple_of(i * 256, 256), 256)
        o = obuf[:, :, :, cols].reshape(2048, 256)
        v = dot(wt[...], o, NN)
        ghb[0, :, cols] = v[:128]
        ghb[1, :, cols] = v[128:]

    ghs[...] = ghb[oth].astype(BF16)
    g_x = send(ghs, ghr, sib)

    for c in ph_near:
        c.wait_recv()

    def second(i):
        for side, block in ((0, up[i]), (1, down[i])):
            s1[i][side].wait_recv()
            pbuf[block, side] = (
                pbuf[block, side].astype(F32) + r1[side, i].astype(F32)
            ).astype(BF16)
        return (
            send(pbuf.at[up[i]], r2.at[0, i], zp), send(pbuf.at[down[i]], r2.at[1, i], zm)
        )

    s2 = [second(0)]

    def to_grad(plane, source):
        @pl.loop(0, 4)
        def _(i):
            cols = pl.ds(pl.multiple_of(i * 256, 256), 256)
            v = (source[:, cols].astype(F32) * der[plane, :, cols]).astype(BF16)
            cg[plane, :, cols] = v
            cgt[plane, cols] = v.astype(F32).T.astype(BF16)

    to_grad(own, ghb.at[own])
    g_x.wait_recv()
    to_grad(oth, ghr)
    g_up = send(cgt.at[1], chalo.at[0], ch, f_up)
    g_dn = send(cgt.at[0], chalo.at[1], ch, f_dn)


    def window_row(plane):
        return jnp.concatenate([x3t[plane, 32 * b : 32 * b + 1024] for b in range(3)], axis=1)

    both = cg[...].reshape(256, 1024)

    def x_slice(f):
        return pl.ds(pl.multiple_of((f // 2) * 288, 32), 288)

    def kernel_chunk(a, value):
        for t in range(9):
            kgb[a, t * 128 : (t + 1) * 128] = value[:, t * 128 : (t + 1) * 128].astype(BF16)
        return [send(kgb.at[a, x_slice(f)], kgr.at[a, fx], ch, f) for f in fxs]

    kgf[...] = dot(both, window_row(1), NN)
    ks = [kernel_chunk(0, kgf[128:] + dot(cg[0], window_row(0), NN))]
    v2 = dot(both, window_row(2), NN)
    ks.append(kernel_chunk(1, kgf[:128] + v2[128:]))
    ks.append(kernel_chunk(2, v2[:128] + dot(cg[1], window_row(3), NN)))

    @pl.loop(0, 8)
    def _(j):
        h = jnp.concatenate([hbuf[0], hbuf[1]], axis=0)
        v = dot(obuf[j].reshape(256, 1024), h, NT)
        lo, hi = v[:, :128], v[:, 128:]
        wgf[j] = jnp.where(co == 0, lo, hi)
        wgs[j] = jnp.where(co == 0, hi, lo).astype(BF16)

    wg_x = send(wgs, wgr, sib)

    def kernel_pair(a):
        total = kgb[a, x_slice(fi)].astype(F32)
        for c in ks[a]:
            c.wait_recv()
        for f in fxs:
            total = total + kgr[a, f // 2].astype(F32)
        kgs[a] = total.astype(BF16)
        return send(kgs.at[a], kgy.at[a], ch, fy)

    ky = [kernel_pair(0)]
    spread(c3t, 1, cgt.at[0], False, one)
    spread(c3t, 2, cgt.at[1], False, one)

    for j, (a0, a1) in enumerate(((1, 2), (0, 1))):
        rows = slice(j * 1152, (j + 1) * 1152)
        kback[rows, 0:128] = k_ref[9 * a0 : 9 * a0 + 9].reshape(1152, 128)
        kback[rows, 128:256] = k_ref[9 * a1 : 9 * a1 + 9].reshape(1152, 128)
    back = (2, 1, 0)

    @pl.loop(0, 4)
    def _(i):
        cols = pl.ds(pl.multiple_of(i * 256, 256), 256)
        wins = windows(c3t, 1, i, back) + windows(c3t, 2, i, back)
        v = dot(jnp.concatenate(wins, axis=1), kback[...], NN)
        ghb[0, :, cols] = v[:, :128].T
        ghb[1, :, cols] = v[:, 128:].T

    ky.append(kernel_pair(1))
    ky.append(kernel_pair(2))
    wg_x.wait_recv()
    wgf[...] = wgf[...] + wgr[...].astype(F32)
    wgp[...] = wgf[...].astype(BF16)

    def f_pair(f):
        return pl.ds((f // 2) * 2, 2)

    wq = [send(wgp.at[f_pair(f)], wgq.at[fx], ch, f) for f in fxs]

    s2.append(second(1))
    kq = []
    for a in range(3):
        ky[a].wait_recv()
        kgall[a, x_slice(fi)] = (kgs[a].astype(F32) + kgy[a].astype(F32)).astype(BF16)
        kq += [
            send(kgall.at[a, x_slice(fi)], kgall.at[a, x_slice(fi)], ch, f) for f in fxs
        ]

    for c in s2[0]:
        c.wait_recv()
    pbuf[here[0]] = (
        pbuf[here[0]].astype(F32) + r2[0, 0].astype(F32) + r2[1, 0].astype(F32)
    ).astype(BF16)
    s3 = send(pbuf.at[here[0]], r3, yn)

    total = wgf[f_pair(fi)]
    for c in wq:
        c.wait_recv()
    for f in fxs:
        total = total + wgq[f // 2].astype(F32)
    wgf[f_pair(fi)] = total
    wgy[...] = wgf[fy].astype(BF16)
    wy = send(wgy, wgz, ch, fy)

    g_up.wait_recv()
    g_dn.wait_recv()
    spread(c3t, 0, chalo.at[0], False, first)
    spread(c3t, 3, chalo.at[1], False, last)

    for plane in range(2):
        @pl.loop(0, 4)
        def _(i):
            cols = pl.ds(pl.multiple_of(i * 256, 256), 256)
            wins = windows(c3t, 3 * plane, i, back)
            taps = k_ref[18 * (1 - plane) : 18 * (1 - plane) + 9].reshape(1152, 128)
            v = dot(jnp.concatenate(wins, axis=1), taps, NN)
            ig_out[:, plane, cols] = (ghb[plane, :, cols] + v.T).astype(BF16)

    ig_store = local(ig_out, ig_res, 4)
    wy.wait_recv()
    wg_out[...] = wgf[fi] + wgz[...].astype(F32)
    stores = [ig_store, local(wg_out, wg_res, 5)]
    for a in range(3):
        for c in kq[3 * a : 3 * a + 3]:
            c.wait_recv()
        kg_out[9 * a : 9 * a + 9] = kgall[a].astype(F32).reshape(9, 128, 128)
        part = pl.ds(9 * a, 9)
        stores.append(local(kg_out.at[part], kg_res.at[part], 6 + a))
    for c in s2[1]:
        c.wait_recv()
    s3.wait_recv()
    for plane in range(2):
        p_out[:, plane] = (
            pbuf[here[1], plane].astype(F32) + r2[0, 1, plane].astype(F32)
            + r2[1, 1, plane].astype(F32) + r3[plane].astype(F32)
        ).astype(BF16)
    stores.append(local(p_out, p_res, 9))
    for c in stores:
        c.wait()
    for c in sent:
        c.wait_send()


def copy_kernel(*refs):
    sem = refs[12]
    loads, stores = [], []
    for i in range(4):
        src, held = refs[i], refs[8 + i]
        step = src.shape[0] // PIECES[i]
        for j in range(PIECES[i]):
            part = pl.ds(j * step, step)
            copy = pltpu.make_async_copy(src.at[part], held.at[part], sem.at[0, len(loads)])
            copy.start()
            loads.append((copy, held.at[part], refs[4 + i].at[part]))
    for copy, held, dst in loads:
        copy.wait()
        stores.append(pltpu.make_async_copy(held, dst, sem.at[1, len(stores)]))
        stores[-1].start()
    for copy in stores:
        copy.wait()


def body(inputs, conv_kernel, proj_weight, out_grad):
    anywhere = pl.BlockSpec(memory_space=pl.ANY)
    shapes = [
        ((128, 2, 1024), BF16),
        ((27, 128, 128), BF16),
        ((256, 128), BF16),
        ((128, 2, 1024), BF16),
        ((2, 1024, 128), BF16),
        ((2, 128, 1024), BF16),
        ((128, 2, 1024), BF16),
        ((128, 2, 1024), BF16),
        ((27, 128, 128), F32),
        ((256, 128), F32),
        ((8, 2, 128, 1024), BF16),
        ((2, 1024, 128), BF16),
        ((4, 1088, 384), BF16),
        ((256, 3456), BF16),
        ((2, 2048, 128), BF16),
        ((256, 2048), BF16),
        ((2, 128, 1024), BF16),
        ((2, 128, 1024), BF16),
        ((2, 128, 1024), F32),
        ((8, 2, 128, 1024), BF16),
        ((8, 128, 1024), BF16),
        ((2, 2, 128, 1024), BF16),
        ((2, 2, 2, 128, 1024), BF16),
        ((2, 128, 1024), BF16),
        ((2, 128, 1024), F32),
        ((128, 1024), BF16),
        ((128, 1024), BF16),
        ((2, 128, 1024), BF16),
        ((2, 1024, 128), BF16),
        ((2, 1024, 128), BF16),
        ((4, 1088, 384), BF16),
        ((2304, 256), BF16),
        ((8, 256, 128), F32),
        ((8, 256, 128), BF16),
        ((8, 256, 128), BF16),
        ((8, 256, 128), BF16),
        ((4, 2, 256, 128), BF16),
        ((256, 128), BF16),
        ((256, 128), BF16),
        ((256, 1152), F32),
        ((3, 1152, 128), BF16),
        ((3, 4, 288, 128), BF16),
        ((3, 288, 128), BF16),
        ((3, 288, 128), BF16),
        ((3, 1152, 128), BF16),
    ]
    out_shape = (
        jax.ShapeDtypeStruct((128, 2, 1024), BF16),
        jax.ShapeDtypeStruct((128, 2, 1024), BF16),
        jax.ShapeDtypeStruct((27, 128, 128), F32),
        jax.ShapeDtypeStruct((256, 128), F32),
    )
    results = pl.pallas_call(
        kernel,
        out_shape=out_shape,
        in_specs=[anywhere] * 4,
        out_specs=(anywhere,) * 4,
        scratch_shapes=[pltpu.VMEM(s, d) for s, d in shapes]
        + [pltpu.SemaphoreType.DMA((N_SEMS,)), pltpu.SemaphoreType.DMA((N_SEMS,)), pltpu.SemaphoreType.DMA((10,))],
        compiler_params=pltpu.CompilerParams(
            collective_id=0, has_side_effects=True, vmem_limit_bytes=56 * 1024 * 1024
        ),
    )(inputs, conv_kernel, proj_weight, out_grad)
    return pl.pallas_call(
        copy_kernel,
        out_shape=out_shape,
        in_specs=[anywhere] * 4,
        out_specs=(anywhere,) * 4,
        scratch_shapes=[pltpu.VMEM(o.shape, o.dtype) for o in out_shape]
        + [pltpu.SemaphoreType.DMA((2, sum(PIECES)))],
    )(*results)


def solution(mesh):
    in_specs = (
        P("chan", "filt", None),
        P(None, "chan", None),
        P("filt", "chan"),
        P("chan", "filt", None),
    )
    out_specs = (
        P("chan", "filt", None),
        P("chan", "filt", None),
        P(None, "chan", None),
        P("filt", "chan"),
    )
    return jax.shard_map(body, mesh=mesh, in_specs=in_specs, out_specs=out_specs, check_vma=False)
```
